128 devices in a mesh: lat: 2 (over z_lo), lon: 64 (over x, y, z_hi, core).
Axes of the slice: x: 4, y: 4, z: 4 (z_hi: 2, z_lo: 2; z = z_hi * 2 + z_lo), core: 2. Of those that a mesh axis runs over, the one named last changes fastest.
Arguments:
- grid_state: bfloat16 [84, 32, 8192], P(None, 'lat', 'lon'), may hold values from -6 to 6
- mesh_feat: bfloat16 [32768, 1024], P(('lat', 'lon')), may hold values from -6 to 6
- enc_src: int32 [16, 32768], P(None, ('lat', 'lon')), may hold values from 0 to 5119, as said below
- enc_count: int32 [32768], P(('lat', 'lon')), may hold values from 1 to 16, as said below
- nbr_ids: int32 [32, 32768], P(None, ('lat', 'lon')), may hold values from 0 to 32767, as said below
- nbr_count: int32 [32768], P(('lat', 'lon')), may hold values from 2 to 32, as said below
- dec_src: int32 [3, 32, 8192], P(None, 'lat', 'lon'), may hold values from 0 to 32767, as said below
- w_embed: bfloat16 [84, 1024], replicated, may hold values from -0.625 to 0.625
- w_encode: bfloat16 [1024, 1024], replicated, may hold values from -0.1875 to 0.1875
- w_query: bfloat16 [1024, 1024], replicated, may hold values from -4 to 4
- w_key: bfloat16 [1024, 1024], replicated, may hold values from -4 to 4
- w_value: bfloat16 [1024, 1024], replicated, may hold values from -0.1875 to 0.1875
- w_output: bfloat16 [1024, 1024], replicated, may hold values from -0.1875 to 0.1875
- w_decode: bfloat16 [1024, 1024], replicated, may hold values from -0.1875 to 0.1875
- w_readout: bfloat16 [1024, 84], replicated, may hold values from -0.1875 to 0.1875
- norm_attn: float32 [1024], replicated, may hold values from 0.5 to 1.5
- norm_dec: float32 [1024], replicated, may hold values from 0.5 to 1.5
Outputs:
- denoised: float32 [84, 32, 8192], P(None, 'lat', 'lon')
The draws below stay inside these ranges and needn't reach their ends.
Inputs may be any that keep to these rules, and one draw needn't show every extreme that they name: `enc_src`: mesh node j belongs to block j // 256, numbered lat index times the number of lon indices plus lon index. Every entry of column j, padding included, names a cell of the window of 160 columns around that lon index's sector, in any row. `enc_count`: some node of every block has 16. `nbr_ids`: slot 0 of node j is j itself. The 32 slots of a node, padding included, are distinct mesh nodes whose block has the same or a cyclically adjacent lon index, and any lat index. `nbr_count`: some node of every block has 32. `dec_src`: the mesh nodes feeding cell (r, c) lie in blocks whose lon index is c // 128 or cyclically adjacent to it, any lat index.
All inputs are finite; a program needn't handle non-finite values.
Results may differ from the reference program's by a relative error of at most 0.0039.
Values may be sent and summed in bfloat16 or wider, within the bound.
A program may use at most 128 MiB of HBM per device.

```python
import math
import jax
import jax.numpy as jnp
from jax import lax

V = 84
D = 1024
HEADS = 16
HEAD_DIM = 64
LAT_DEV = 16
LON_DEV = 128
HALO = 16
M_DEV = 256
KE = 16
KM = 32
LATS = 32
LONS = 8192
MESH = 32768
N_LAT = 2
N_LON = 64


def window_to_node(position, sector):
    band_index = position // (3 * M_DEV)
    offset = position // M_DEV % 3
    member = position % M_DEV
    return ((band_index * N_LON + (sector + offset - 1) % N_LON) * M_DEV + member).astype(jnp.int32)


def draw_enc_src(key, part):
    key = jax.random.fold_in(key, 101)
    node_total = M_DEV * N_LAT * N_LON
    row_key, col_key = jax.random.split(key)
    row_ids = jax.random.randint(row_key, (KE, node_total), 0, LAT_DEV * N_LAT)
    places = jax.random.randint(col_key, (KE, node_total), 0, LON_DEV + 2 * HALO)
    return (row_ids * (LON_DEV + 2 * HALO) + places).astype(jnp.int32)


def draw_enc_count(key, part):
    key = jax.random.fold_in(key, 102)
    node_total = M_DEV * N_LAT * N_LON
    counts = jax.random.randint(key, (node_total,), 1, KE + 1)
    return counts.at[::M_DEV].set(KE).astype(jnp.int32)


def draw_nbr_ids(key, part):
    key = jax.random.fold_in(key, 103)
    node_total = M_DEV * N_LAT * N_LON
    node_ids = jnp.arange(node_total, dtype=jnp.int32)
    device = node_ids // M_DEV
    band_index = device // N_LON
    sector = device % N_LON
    window = 3 * N_LAT * M_DEV
    stride = window // KM
    own_slot = (band_index * 3 + 1) * M_DEV + node_ids % M_DEV
    slot_index = jnp.arange(KM, dtype=jnp.int32)[:, None]
    jitter = jax.random.randint(key, (KM, node_total), 0, stride)
    offsets = jnp.where(slot_index == 0, 0, slot_index * stride + jitter)
    position = (own_slot[None, :] + offsets) % window
    return window_to_node(position, sector[None, :])


def draw_nbr_count(key, part):
    key = jax.random.fold_in(key, 104)
    node_total = M_DEV * N_LAT * N_LON
    counts = jax.random.randint(key, (node_total,), 2, KM + 1)
    return counts.at[::M_DEV].set(KM).astype(jnp.int32)


def draw_dec_src(key, part):
    key = jax.random.fold_in(key, 105)
    lat_total = LAT_DEV * N_LAT
    lon_total = LON_DEV * N_LON
    sector = (jnp.arange(lon_total, dtype=jnp.int32) // LON_DEV)[None, None, :]
    position = jax.random.randint(key, (3, lat_total, lon_total), 0, 3 * N_LAT * M_DEV)
    return window_to_node(position, sector)


def shared_projection(key, which):
    base_key = jax.random.fold_in(key, 107)
    own_part = jax.random.truncated_normal(jax.random.fold_in(base_key, which), -4.0, 4.0, (D, D), jnp.float32) / math.sqrt(D)
    return own_part


def draw_w_query(key, part):
    return shared_projection(key, 1).astype(jnp.bfloat16)


def draw_w_key(key, part):
    return shared_projection(key, 2).astype(jnp.bfloat16)


def level_of(stream_key, shape, cuts, smallest, largest):
    factor_of, own = 1.0, jax.random.fold_in(stream_key, 6)
    for dim, shards_of in cuts:
        draws = jnp.exp(jax.random.uniform(jax.random.fold_in(own, dim), (shards_of,), jnp.float32, smallest / len(cuts), largest / len(cuts)))
        factor_of = factor_of * jnp.repeat(draws, shape[dim] // shards_of).reshape([-1 if axis == dim else 1 for axis in range(len(shape))])
    return factor_of


def bell_draw(own_key, extent, deviation, reach, cuts=(), held_as=jnp.bfloat16):
    loudness = level_of(own_key, extent, cuts, -0.22, 0.18) if cuts else 1.0
    result = jax.random.normal(own_key, extent, jnp.float32) * deviation * loudness
    return jnp.minimum(jnp.maximum(result, -reach), reach).astype(held_as)


def setup_inputs(seed: int = 0) -> dict:
    splits = jax.random.split(jax.random.key(seed), 18)
    return {
        "grid_state": bell_draw(splits[0], (V, LATS, LONS), 1.0, 6.0, ((1, 2), (2, 64))),
        "mesh_feat": bell_draw(splits[1], (MESH, D), 1.0, 6.0, ((0, 128),)),
        "enc_src": draw_enc_src(jax.random.fold_in(splits[17], 71), 0),
        "enc_count": draw_enc_count(jax.random.fold_in(splits[17], 71), 0),
        "nbr_ids": draw_nbr_ids(jax.random.fold_in(splits[17], 71), 0),
        "nbr_count": draw_nbr_count(jax.random.fold_in(splits[17], 71), 0),
        "dec_src": draw_dec_src(jax.random.fold_in(splits[17], 71), 0),
        "w_embed": bell_draw(splits[7], (V, D), V ** -0.5, 0.625),
        "w_encode": bell_draw(splits[8], (D, D), D ** -0.5, 0.1875),
        "w_query": draw_w_query(jax.random.fold_in(splits[17], 71), 0),
        "w_key": draw_w_key(jax.random.fold_in(splits[17], 71), 0),
        "w_value": bell_draw(splits[11], (D, D), D ** -0.5, 0.1875),
        "w_output": bell_draw(splits[12], (D, D), D ** -0.5, 0.1875),
        "w_decode": bell_draw(splits[13], (D, D), D ** -0.5, 0.1875),
        "w_readout": bell_draw(splits[14], (D, V), D ** -0.5, 0.1875),
        "norm_attn": jnp.clip(1.0 + 0.1 * jax.random.normal(splits[15], (D,), jnp.float32), 0.5, 1.5),
        "norm_dec": jnp.clip(1.0 + 0.1 * jax.random.normal(splits[16], (D,), jnp.float32), 0.5, 1.5),
    }


def layer_norm(inputs_f, gain):
    centre = inputs_f - lax.optimization_barrier(jnp.mean(inputs_f, axis=-1, keepdims=True))
    spread = lax.optimization_barrier(jnp.mean(centre * centre, axis=-1, keepdims=True))
    return centre * lax.rsqrt(spread + 1e-05) * gain

def reference(grid_state, mesh_feat, enc_src, enc_count, nbr_ids, nbr_count, dec_src, w_embed, w_encode, w_query, w_key, w_value, w_output, w_decode, w_readout, norm_attn, norm_dec):
    lat_total = LAT_DEV * N_LAT
    lon_total = LON_DEV * N_LON
    block_count = N_LAT * N_LON
    node_total = M_DEV * block_count
    span_cols = LON_DEV + 2 * HALO
    flat_grid = grid_state.reshape(V, lat_total * lon_total)

    def encode_block(operands):
        source_block, count_block, block_id = operands
        sector = block_id % N_LON
        row_ids = source_block // span_cols
        col_ids = (sector * LON_DEV + source_block % span_cols - HALO) % lon_total
        cells = (row_ids * lon_total + col_ids).astype(jnp.int32)
        picked = jnp.take(flat_grid, cells, axis=1).astype(jnp.float32)
        live_slot = jnp.arange(KE, dtype=jnp.int32)[:, None] < count_block[None, :]
        summed = lax.optimization_barrier(jnp.sum(jnp.where(live_slot[None], picked, 0.0), axis=1))
        return summed / count_block.astype(jnp.float32)[None, :]
    sources = enc_src.reshape(KE, block_count, M_DEV).transpose(1, 0, 2)
    counts = enc_count.reshape(block_count, M_DEV)
    block_ids = jnp.arange(block_count, dtype=jnp.int32)
    mean_cells = lax.map(encode_block, (sources, counts, block_ids))
    mean_cells = mean_cells.transpose(1, 0, 2).reshape(V, node_total).astype(jnp.bfloat16)
    embedded = jax.nn.silu(jnp.dot(mean_cells.T, w_embed, preferred_element_type=jnp.float32)).astype(jnp.bfloat16)
    latent = mesh_feat.astype(jnp.float32) + jnp.dot(embedded, w_encode, preferred_element_type=jnp.float32)
    normed = layer_norm(latent, norm_attn).astype(jnp.bfloat16)
    queries = jnp.dot(normed, w_query, preferred_element_type=jnp.float32).astype(jnp.bfloat16)
    key_rows = jnp.dot(normed, w_key, preferred_element_type=jnp.float32).astype(jnp.bfloat16)
    value_rows = jnp.dot(normed, w_value, preferred_element_type=jnp.float32).astype(jnp.bfloat16)
    score_scale = HEAD_DIM ** (-0.5)

    def attend(operands):
        query_block, index_block, count_block = operands
        live_slot = jnp.arange(KM, dtype=jnp.int32)[:, None] < count_block[None, :]
        near_keys = jnp.take(key_rows, index_block, axis=0).astype(jnp.float32).reshape(KM, M_DEV, HEADS, HEAD_DIM)
        near_values = jnp.take(value_rows, index_block, axis=0).astype(jnp.float32).reshape(KM, M_DEV, HEADS, HEAD_DIM)
        query_heads = query_block.astype(jnp.float32).reshape(M_DEV, HEADS, HEAD_DIM)
        scores = jnp.einsum('bhd,kbhd->kbh', query_heads, near_keys) * score_scale
        scores = jnp.where(live_slot[:, :, None], scores, -jnp.inf)
        peak_score = lax.optimization_barrier(jnp.max(scores, axis=0, keepdims=True))
        expo_score = jnp.where(live_slot[:, :, None], jnp.exp(scores - peak_score), 0.0)
        weights = (expo_score / lax.optimization_barrier(jnp.sum(expo_score, axis=0, keepdims=True))).astype(jnp.bfloat16)
        context = jnp.einsum('kbh,kbhd->bhd', weights.astype(jnp.float32), near_values)
        return context.astype(jnp.bfloat16).reshape(M_DEV, D)
    query_blocks = queries.reshape(block_count, M_DEV, D)
    index_blocks = nbr_ids.reshape(KM, block_count, M_DEV).transpose(1, 0, 2)
    count_blocks = nbr_count.reshape(block_count, M_DEV)
    context = lax.map(attend, (query_blocks, index_blocks, count_blocks)).reshape(node_total, D)
    mixed = latent + jnp.dot(context, w_output, preferred_element_type=jnp.float32)
    normed_out = layer_norm(mixed, norm_dec).astype(jnp.bfloat16)
    decoded = jax.nn.silu(jnp.dot(normed_out, w_decode, preferred_element_type=jnp.float32)).astype(jnp.bfloat16)
    readout = jnp.dot(decoded, w_readout, preferred_element_type=jnp.float32).astype(jnp.bfloat16).T

    def decode_row(index_row):
        picked = jnp.take(readout, index_row, axis=1).astype(jnp.float32)
        return lax.optimization_barrier(jnp.sum(picked, axis=1)) / 3.0
    update = lax.map(decode_row, dec_src.transpose(1, 0, 2))
    return grid_state.astype(jnp.float32) + update.transpose(1, 0, 2)
```

```python
import jax
import jax.numpy as jnp
from jax import lax
from jax.experimental import pallas as pl
from jax.experimental.pallas import tpu as pltpu
from jax.sharding import PartitionSpec as P

f32, bf16, i32 = jnp.float32, jnp.bfloat16, jnp.int32
MESH = pl.DeviceIdType.MESH
V = 84
D = 1024
NB = 256
KE = 16
KM = 32
ROWS = 16
COLS = 128
HALO = 16
SLOTS = 6
WINDOW = SLOTS * NB
SECTORS = 64
CHUNKS = 4
CHUNK = NB // CHUNKS
NEG = -1e30


def tile16(row):
    return jnp.broadcast_to(row, (16, row.shape[1])).astype(bf16)


def rep(tile, times):
    return jnp.concatenate([tile] * times, axis=0)


def row_codes(rows, cols, base=0):
    return (lax.broadcasted_iota(i32, (rows, cols), 0) + base).astype(f32).astype(bf16)


def flag(mask):
    return jnp.where(mask, jnp.ones((), bf16), jnp.zeros((), bf16))


def slot_of(node, lat, lon, inner):
    member = (node & (NB - 1)).astype(f32)
    device = node >> 8
    far = (device >> 6) ^ lat
    sector = device & (SECTORS - 1)
    slot = jnp.where(sector == lon, 2 * far, jnp.where(sector == inner, 1 + 2 * far, 5 - far))
    return slot.astype(f32), member


def build_enc(src, count, lat, parity, lo_ref, hi_ref, onehot_ref, a_ref):
    row = (src * 6554) >> 20
    place = src - row * (COLS + 2 * HALO)
    far = (row >> 4) ^ lat
    r = row & (ROWS - 1)
    west = place < HALO
    east = place >= HALO + COLS
    halo = west | east
    c = jnp.where(east, place - (HALO + COLS), place)
    side = jnp.where(east, 1, 0)
    outer = side ^ (1 - parity)
    hi = jnp.where(halo, 32 + 4 * far + 2 * outer + (r >> 3), 16 * far + r)
    lo = jnp.where(halo, (r & 7) * HALO + c, place - HALO)
    live = lax.broadcasted_iota(i32, src.shape, 0) < count
    hi_ref[...] = jnp.where(live, hi, -1).astype(f32)
    lo_ref[...] = lo.astype(f32)
    iota = row_codes(COLS, NB)
    for s in range(KE):
        onehot_ref[s * COLS : (s + 1) * COLS, :] = flag(iota == rep(tile16(lo_ref[s : s + 1, :]), 8))

    def group(g, carry):
        code = g.astype(f32)
        acc = jnp.zeros((COLS, NB), bf16)
        for s in range(KE):
            hit = tile16(jnp.where(hi_ref[s : s + 1, :] == code, 1.0, 0.0))
            acc = acc + onehot_ref[s * COLS : (s + 1) * COLS, :] * rep(hit, 8)
        a_ref[pl.ds(pl.multiple_of(g * COLS, COLS), COLS), :] = acc
        return carry

    lax.fori_loop(0, 40, group, 0)


def build_mask(ids, count, lat, lon, inner, hi_ref, lo_ref, hit_ref, member_ref, bias_ref):
    slot, member = slot_of(ids, lat, lon, inner)
    live = lax.broadcasted_iota(i32, ids.shape, 0) < count
    hi_ref[...] = jnp.where(live, slot, -1.0)
    lo_ref[...] = member
    for s in range(KM):
        for b in range(SLOTS):
            at = (s * SLOTS + b) * 16
            hit_ref[at : at + 16, :] = tile16(jnp.where(hi_ref[s : s + 1, :] == float(b), 1.0, 0.0))
    step = 32

    def chunk(c, carry):
        iota = row_codes(step, NB, c * step)
        acc = [jnp.zeros((step, NB), bf16) for _ in range(SLOTS)]
        for s in range(KM):
            one = flag(iota == rep(tile16(lo_ref[s : s + 1, :]), step // 16))
            for b in range(SLOTS):
                at = (s * SLOTS + b) * 16
                acc[b] = acc[b] + one * rep(hit_ref[at : at + 16, :], step // 16)
        for b in range(SLOTS):
            member_ref[b, pl.ds(pl.multiple_of(c * step, step), step), :] = acc[b]
        return carry

    lax.fori_loop(0, NB // step, chunk, 0)
    for b in range(SLOTS):
        seen = member_ref[b].astype(f32).T
        bias_ref[:, b * NB : (b + 1) * NB] = jnp.where(seen > 0.0, 0.0, NEG)


def build_dec(src_ref, lat, lon, inner, pick_ref):
    def chunk(c, carry):
        for half in range(2):
            lanes = slice(half * COLS, (half + 1) * COLS)
            codes = []
            for i in range(3):
                ids = src_ref[i, pl.ds(c * 2 + half, 1), :]
                slot, member = slot_of(ids, lat, lon, inner)
                hits = [tile16(jnp.where(slot == float(b), 1.0, 0.0)) for b in range(SLOTS)]
                codes.append((tile16(member), hits))
            for k in range(4):
                iota = row_codes(64, COLS, k * 64)
                ones = [flag(iota == rep(member, 4)) for member, _ in codes]
                for b in range(SLOTS):
                    at = b * NB + k * 64
                    pick_ref[c, at : at + 64, lanes] = (
                        ones[0] * rep(codes[0][1][b], 4)
                        + ones[1] * rep(codes[1][1][b], 4)
                        + ones[2] * rep(codes[2][1][b], 4)
                    )
        return carry

    lax.fori_loop(0, 8, chunk, 0)


def silu(u):
    return u * jax.nn.sigmoid(u)


def layer_norm(x, gain):
    centre = x - jnp.mean(x, axis=-1, keepdims=True)
    spread = jnp.mean(centre * centre, axis=-1, keepdims=True)
    return centre * lax.rsqrt(spread + 1e-05) * gain


def dot(a, b):
    return jnp.dot(a, b, preferred_element_type=f32)


def attention(q_ref, k_ref, v_ref, bias_ref, c_ref):
    low = lax.broadcasted_iota(i32, (1, 128), 1) < 64
    one, zero = jnp.ones((), bf16), jnp.zeros((), bf16)

    def pair(p, carry):
        cols = pl.ds(pl.multiple_of(p * 128, 128), 128)
        keys = k_ref[:, cols]
        values = v_ref[:, cols]
        query = q_ref[:, cols]
        outs = []
        for half in range(2):
            own = low if half == 0 else jnp.logical_not(low)
            scores = lax.dot_general(
                jnp.where(own, query, zero), keys, (((1,), (1,)), ((), ())), preferred_element_type=f32
            )
            scores = scores + bias_ref[...]
            peak = jnp.max(scores, axis=1, keepdims=True)
            expo = jnp.exp(scores - peak).astype(bf16)
            outs.append(dot(expo, jnp.where(own, values, one)))
        total = pltpu.roll(jnp.where(low, outs[1], outs[0]), 64, 1)
        c_ref[:, cols] = (jnp.where(low, outs[0], outs[1]) / total).astype(bf16)
        return carry

    lax.fori_loop(0, D // 128, pair, 0)


def kernel(
    grid_ref,
    mesh_ref,
    enc_src_ref,
    enc_count_ref,
    nbr_ref,
    nbr_count_ref,
    dec_src_ref,
    w_embed_ref,
    w_encode_hbm,
    w_query_hbm,
    w_key_hbm,
    w_value_hbm,
    w_output_hbm,
    w_decode_hbm,
    w_readout_ref,
    gain_attn_ref,
    gain_dec_ref,
    out_ref,
    halo_ref,
    mesh_w,
    mean_w,
    read_w,
    weights,
    enc_lo,
    enc_hi,
    enc_onehot,
    enc_pick,
    nbr_hi,
    nbr_lo,
    nbr_hit,
    nbr_member,
    bias_ref,
    dec_pick,
    latent_ref,
    query_ref,
    key_ref,
    value_ref,
    context_ref,
    local_sem,
    send_sem,
    recv_sem,
):
    lat = lax.axis_index("lat")
    lon = lax.axis_index("lon")
    parity = lax.rem(lon, 2)
    inner = lon + 1 - 2 * parity
    outer = lax.rem(lon + 2 * parity - 1 + SECTORS, SECTORS)
    core = (lat, inner)
    band = (1 - lat, lon)
    band_core = (1 - lat, inner)
    far = (1 - lat, outer)
    near = (lat, outer)

    loads = [
        pltpu.make_async_copy(source, weights.at[i], local_sem.at[i])
        for i, source in enumerate(
            (w_encode_hbm, w_query_hbm, w_key_hbm, w_value_hbm, w_output_hbm, w_decode_hbm)
        )
    ]
    own_load = pltpu.make_async_copy(mesh_ref, mesh_w.at[0], local_sem.at[6])

    barrier = pltpu.get_barrier_semaphore()
    for peer in (core, band, band_core, far, near):
        pl.semaphore_signal(barrier, inc=1, device_id=peer, device_id_type=MESH)
    pl.semaphore_wait(barrier, 5)

    number = iter(range(64))

    def remote(source, target, peer):
        i = next(number)
        return pltpu.make_async_remote_copy(
            src_ref=source,
            dst_ref=target,
            send_sem=send_sem.at[i],
            recv_sem=recv_sem.at[i],
            device_id=peer,
            device_id_type=MESH,
        )

    main = ROWS * COLS
    edge = ROWS * HALO
    inner_edge = pl.ds(pl.multiple_of(main + edge * (1 - parity), edge), edge)
    outer_edge = pl.ds(pl.multiple_of(main + edge * parity, edge), edge)

    def landing(i):
        return halo_ref.at[:, main + i * edge : main + (i + 1) * edge]

    grids = [
        remote(grid_ref.at[:, inner_edge], landing(0), core),
        remote(grid_ref.at[:, outer_edge], landing(1), near),
        remote(grid_ref.at[:, inner_edge], landing(2), band_core),
        remote(grid_ref.at[:, outer_edge], landing(3), far),
        remote(grid_ref.at[:, 0:main], halo_ref.at[:, 0:main], band),
    ]
    for copy in grids:
        copy.start()

    def piece(c):
        return pl.ds(c * CHUNK, CHUNK)

    to_core = remote(mesh_ref, mesh_w.at[1], core)
    to_band = [remote(mesh_ref.at[piece(c)], mesh_w.at[2, piece(c)], band) for c in range(CHUNKS)]
    to_far = [remote(mesh_ref.at[piece(c)], mesh_w.at[4, piece(c)], far) for c in range(CHUNKS)]
    on_core = [
        remote(mesh_w.at[2, piece(c)], mesh_w.at[3, piece(c)], core) for c in range(CHUNKS)
    ]
    on_near = [remote(mesh_w.at[4, piece(0)], mesh_w.at[5, piece(0)], band)] + [
        remote(mesh_w.at[2, piece(c)], mesh_w.at[5, piece(c)], far) for c in range(1, CHUNKS)
    ]
    means = [
        remote(mean_w.at[0], mean_w.at[slot], peer)
        for slot, peer in enumerate((core, band, band_core, far, near), 1)
    ]
    reads = [
        remote(read_w.at[:, 0:NB], read_w.at[:, slot * NB : (slot + 1) * NB], peer)
        for slot, peer in enumerate((core, band, band_core, far, near), 1)
    ]
    for c in range(CHUNKS):
        to_far[c].start()
        to_band[c].start()
    to_core.start()
    own_load.start()
    for load in loads:
        load.start()

    build_enc(enc_src_ref[...], enc_count_ref[...], lat, parity, enc_lo, enc_hi, enc_onehot, enc_pick)
    build_mask(
        nbr_ref[...], nbr_count_ref[...], lat, lon, inner, nbr_hi, nbr_lo, nbr_hit, nbr_member, bias_ref
    )
    for copy in grids:
        copy.wait_recv()
    summed = (
        dot(grid_ref[:, 0:main], enc_pick[0:main, :])
        + dot(halo_ref[:, 0:main], enc_pick[main : 2 * main, :])
        + dot(halo_ref[:, main:], enc_pick[2 * main :, :])
    )
    mean_w[0] = (summed / enc_count_ref[...].astype(f32)).astype(bf16)
    for copy in means:
        copy.start()

    own_load.wait()
    for load in loads:
        load.wait()

    def block(b, carry):
        @pl.when(b == 1)
        def _():
            means[0].wait_recv()
            to_core.wait_recv()
            to_far[0].wait_recv()
            on_near[0].start()
            for c in range(CHUNKS):
                to_band[c].wait_recv()
                on_core[c].start()
                if c:
                    on_near[c].start()

        @pl.when(b == 2)
        def _():
            means[1].wait_recv()

        @pl.when(b == 3)
        def _():
            means[2].wait_recv()
            for copy in on_core:
                copy.wait_recv()

        @pl.when(b == 4)
        def _():
            means[3].wait_recv()
            for copy in to_far[1:]:
                copy.wait_recv()

        @pl.when(b == 5)
        def _():
            means[4].wait_recv()
            for copy in on_near:
                copy.wait_recv()

        embedded = silu(
            lax.dot_general(
                mean_w[b], w_embed_ref[...], (((0,), (0,)), ((), ())), preferred_element_type=f32
            )
        ).astype(bf16)
        latent = mesh_w[b].astype(f32) + dot(embedded, weights[0])
        normed = layer_norm(latent, gain_attn_ref[...]).astype(bf16)
        rows = pl.ds(pl.multiple_of(b * NB, NB), NB)
        key_ref[rows, :] = dot(normed, weights[2]).astype(bf16)
        value_ref[rows, :] = dot(normed, weights[3]).astype(bf16)

        @pl.when(b == 0)
        def _():
            latent_ref[...] = latent
            query_ref[...] = (dot(normed, weights[1]).astype(bf16).astype(f32) * 0.125).astype(bf16)

        return carry

    lax.fori_loop(0, SLOTS, block, 0)

    attention(query_ref, key_ref, value_ref, bias_ref, context_ref)
    mixed = latent_ref[...] + dot(context_ref[...], weights[4])
    normed_out = layer_norm(mixed, gain_dec_ref[...]).astype(bf16)
    decoded = silu(dot(normed_out, weights[5])).astype(bf16)
    read_w[:, 0:NB] = lax.dot_general(
        w_readout_ref[...], decoded, (((0,), (1,)), ((), ())), preferred_element_type=f32
    ).astype(bf16)
    for copy in reads:
        copy.start()
    build_dec(dec_src_ref, lat, lon, inner, dec_pick)
    for copy in reads:
        copy.wait_recv()

    def finish(c, carry):
        lanes = pl.ds(pl.multiple_of(c * NB, NB), NB)
        update = dot(read_w[...], dec_pick[c])
        out_ref[:, lanes] = grid_ref[:, lanes].astype(f32) + update / 3.0
        return carry

    lax.fori_loop(0, main // NB, finish, 0)
    for copy in grids + [to_core] + to_band + to_far + on_core + on_near + means + reads:
        copy.wait_send()


def body(
    grid_state,
    mesh_feat,
    enc_src,
    enc_count,
    nbr_ids,
    nbr_count,
    dec_src,
    w_embed,
    w_encode,
    w_query,
    w_key,
    w_value,
    w_output,
    w_decode,
    w_readout,
    norm_attn,
    norm_dec,
):
    main = ROWS * COLS
    packed = jnp.concatenate(
        [
            grid_state.reshape(V, main),
            grid_state[:, :, :HALO].reshape(V, ROWS * HALO),
            grid_state[:, :, COLS - HALO :].reshape(V, ROWS * HALO),
        ],
        axis=1,
    )
    vmem = pl.BlockSpec(memory_space=pltpu.VMEM)
    hbm = pl.BlockSpec(memory_space=pl.ANY)
    out = pl.pallas_call(
        kernel,
        out_shape=jax.ShapeDtypeStruct((V, main), f32),
        in_specs=[vmem, hbm] + [vmem] * 6 + [hbm] * 6 + [vmem] * 3,
        out_specs=vmem,
        scratch_shapes=[
            pltpu.VMEM((V, main + 4 * ROWS * HALO), bf16),
            pltpu.VMEM((SLOTS, NB, D), bf16),
            pltpu.VMEM((SLOTS, V, NB), bf16),
            pltpu.VMEM((V, WINDOW), bf16),
            pltpu.VMEM((6, D, D), bf16),
            pltpu.VMEM((KE, NB), f32),
            pltpu.VMEM((KE, NB), f32),
            pltpu.VMEM((KE * COLS, NB), bf16),
            pltpu.VMEM((40 * COLS, NB), bf16),
            pltpu.VMEM((KM, NB), f32),
            pltpu.VMEM((KM, NB), f32),
            pltpu.VMEM((KM * SLOTS * 16, NB), bf16),
            pltpu.VMEM((SLOTS, NB, NB), bf16),
            pltpu.VMEM((NB, WINDOW), f32),
            pltpu.VMEM((8, WINDOW, NB), bf16),
            pltpu.VMEM((NB, D), f32),
            pltpu.VMEM((NB, D), bf16),
            pltpu.VMEM((WINDOW, D), bf16),
            pltpu.VMEM((WINDOW, D), bf16),
            pltpu.VMEM((NB, D), bf16),
            pltpu.SemaphoreType.DMA((7,)),
            pltpu.SemaphoreType.DMA((64,)),
            pltpu.SemaphoreType.DMA((64,)),
        ],
        compiler_params=pltpu.CompilerParams(
            collective_id=0, has_side_effects=True, vmem_limit_bytes=64 * 1024 * 1024 - 65536
        ),
        name="denoise",
    )(
        packed,
        mesh_feat,
        enc_src,
        enc_count.reshape(1, NB),
        nbr_ids,
        nbr_count.reshape(1, NB),
        dec_src,
        w_embed,
        w_encode,
        w_query,
        w_key,
        w_value,
        w_output,
        w_decode,
        w_readout,
        norm_attn.reshape(1, D),
        norm_dec.reshape(1, D),
    )
    return out.reshape(V, ROWS, COLS)


def solution(mesh):
    in_specs = (
        P(None, "lat", "lon"),
        P(("lat", "lon"), None),
        P(None, ("lat", "lon")),
        P(("lat", "lon")),
        P(None, ("lat", "lon")),
        P(("lat", "lon")),
        P(None, "lat", "lon"),
    ) + (P(),) * 10
    return jax.shard_map(
        body, mesh=mesh, in_specs=in_specs, out_specs=P(None, "lat", "lon"), check_vma=False
    )
```

```python
import jax
import jax.numpy as jnp
from jax import lax
from jax.experimental import pallas as pl
from jax.experimental.pallas import tpu as pltpu
from jax.sharding import PartitionSpec as P

f32, bf16, i32 = jnp.float32, jnp.bfloat16, jnp.int32
MESH = pl.DeviceIdType.MESH
V = 84
D = 1024
NB = 256
KE = 16
KM = 32
ROWS = 16
COLS = 128
HALO = 16
SLOTS = 6
WINDOW = SLOTS * NB
SECTORS = 64
CHUNKS = 4
CHUNK = NB // CHUNKS
HEADS = 16
HEAD = 64
VROWS = 80
HALF = WINDOW // 2
NEG = -1e30


def tile16(row):
    return jnp.broadcast_to(row, (16, row.shape[1])).astype(bf16)


def rep(tile, times):
    return jnp.concatenate([tile] * times, axis=0)


def row_codes(rows, cols, base=0):
    return (lax.broadcasted_iota(i32, (rows, cols), 0) + base).astype(f32).astype(bf16)


def flag(mask):
    return jnp.where(mask, jnp.ones((), bf16), jnp.zeros((), bf16))


def slot_of(node, lat, lon, inner):
    member = (node & (NB - 1)).astype(f32)
    device = node >> 8
    far = (device >> 6) ^ lat
    sector = device & (SECTORS - 1)
    slot = jnp.where(sector == lon, 3 * far, jnp.where(sector == inner, 1 + 3 * far, 5 - 3 * far))
    return slot.astype(f32), member


def build_enc(src, count, lat, parity, lo_ref, hi_ref, onehot_ref, a_ref):
    row = (src * 6554) >> 20
    place = src - row * (COLS + 2 * HALO)
    far = (row >> 4) ^ lat
    r = row & (ROWS - 1)
    west = place < HALO
    east = place >= HALO + COLS
    halo = west | east
    c = jnp.where(east, place - (HALO + COLS), place)
    side = jnp.where(east, 1, 0)
    outer = side ^ (1 - parity)
    hi = jnp.where(halo, 32 + 4 * far + 2 * outer + (r >> 3), 16 * far + r)
    lo = jnp.where(halo, (r & 7) * HALO + c, place - HALO)
    live = lax.broadcasted_iota(i32, src.shape, 0) < count
    hi_ref[...] = jnp.where(live, hi, -1).astype(f32)
    lo_ref[...] = lo.astype(f32)
    iota = row_codes(COLS, NB)
    for s in range(KE):
        onehot_ref[s * COLS : (s + 1) * COLS, :] = flag(iota == rep(tile16(lo_ref[s : s + 1, :]), 8))

    def group(g, carry):
        code = g.astype(f32)
        acc = jnp.zeros((COLS, NB), bf16)
        for s in range(KE):
            hit = tile16(jnp.where(hi_ref[s : s + 1, :] == code, 1.0, 0.0))
            acc = acc + onehot_ref[s * COLS : (s + 1) * COLS, :] * rep(hit, 8)
        a_ref[pl.ds(pl.multiple_of(g * COLS, COLS), COLS), :] = acc
        return carry

    lax.fori_loop(0, 40, group, 0)


def build_mask(ids, count, lat, lon, inner, hi_ref, lo_ref, hit_ref, bias_ref):
    slot, member = slot_of(ids, lat, lon, inner)
    live = lax.broadcasted_iota(i32, ids.shape, 0) < count
    hi_ref[...] = jnp.where(live, slot, -1.0)
    lo_ref[...] = member
    for s in range(KM):
        for b in range(SLOTS):
            at = (s * SLOTS + b) * 16
            hit_ref[at : at + 16, :] = tile16(jnp.where(hi_ref[s : s + 1, :] == float(b), 1.0, 0.0))
    step = 32

    def chunk(c, carry):
        iota = row_codes(step, NB, c * step)
        acc = [jnp.zeros((step, NB), bf16) for _ in range(SLOTS)]
        for s in range(KM):
            one = flag(iota == rep(tile16(lo_ref[s : s + 1, :]), step // 16))
            for b in range(SLOTS):
                at = (s * SLOTS + b) * 16
                acc[b] = acc[b] + one * rep(hit_ref[at : at + 16, :], step // 16)
        for b in range(SLOTS):
            rows = pl.ds(pl.multiple_of(b * NB + c * step, step), step)
            bias_ref[rows, :] = jnp.where(acc[b].astype(f32) > 0.0, 0.0, NEG)
        return carry

    lax.fori_loop(0, NB // step, chunk, 0)


def build_dec(src_ref, lat, lon, inner, pick_ref):
    def chunk(c, carry):
        for half in range(2):
            lanes = slice(half * COLS, (half + 1) * COLS)
            codes = []
            for i in range(3):
                ids = src_ref[i, pl.ds(c * 2 + half, 1), :]
                slot, member = slot_of(ids, lat, lon, inner)
                hits = [tile16(jnp.where(slot == float(b), 1.0, 0.0)) for b in range(SLOTS)]
                codes.append((tile16(member), hits))
            for k in range(4):
                iota = row_codes(64, COLS, k * 64)
                ones = [flag(iota == rep(member, 4)) for member, _ in codes]
                for b in range(SLOTS):
                    at = b * NB + k * 64
                    pick_ref[c, at : at + 64, lanes] = (
                        ones[0] * rep(codes[0][1][b], 4)
                        + ones[1] * rep(codes[1][1][b], 4)
                        + ones[2] * rep(codes[2][1][b], 4)
                    )
        return carry

    lax.fori_loop(0, 8, chunk, 0)


def silu(u):
    return u * jax.nn.sigmoid(u)


def layer_norm(x, gain):
    centre = x - jnp.mean(x, axis=-1, keepdims=True)
    spread = jnp.mean(centre * centre, axis=-1, keepdims=True)
    return centre * lax.rsqrt(spread + 1e-05) * gain


def dot(a, b):
    return jnp.dot(a, b, preferred_element_type=f32)


def attention(part, q_ref, k_ref, v_ref, bias_ref, score_refs, expo_refs, sum_ref, peak_ref, midway):
    low = lax.broadcasted_iota(i32, (1, 128), 1) < 64
    zero = jnp.zeros((), bf16)
    span = pl.ds(pl.multiple_of(part * HALF, HALF), HALF)

    def scores(p, half):
        cols = pl.ds(pl.multiple_of(p * 128, 128), 128)
        own = low if half == 0 else jnp.logical_not(low)
        score_refs[half][...] = lax.dot_general(
            k_ref[span, cols],
            jnp.where(own, q_ref[:, cols], zero),
            (((1,), (1,)), ((), ())),
            preferred_element_type=f32,
        )

    def weigh(h, half):
        masked = score_refs[half][...] + bias_ref[span, :]
        peak = jnp.max(masked, axis=0, keepdims=True)
        expo_refs[half][...] = jnp.exp(masked - peak).astype(bf16)
        peak_ref[part, pl.ds(h, 1), :] = peak

    def gather(h, half):
        rows = pl.ds(pl.multiple_of(h * VROWS, 16), VROWS)
        sum_ref[part, h] = dot(v_ref[rows, span], expo_refs[half][...])

    scores(0, 0)

    def pair(p, carry):
        midway(p)
        scores(p, 1)
        gather(jnp.maximum(2 * p - 1, 0), 1)
        weigh(2 * p, 0)
        scores(jnp.minimum(p + 1, HEADS // 2 - 1), 0)
        gather(2 * p, 0)
        weigh(2 * p + 1, 1)
        return carry

    lax.fori_loop(0, HEADS // 2, pair, 0)
    gather(HEADS - 1, 1)


def kernel(
    grid_ref,
    mesh_ref,
    enc_src_ref,
    enc_count_ref,
    nbr_ref,
    nbr_count_ref,
    dec_src_ref,
    w_embed_ref,
    w_encode_hbm,
    w_query_hbm,
    w_key_hbm,
    w_value_hbm,
    w_output_hbm,
    w_decode_hbm,
    w_readout_ref,
    gain_attn_ref,
    gain_dec_ref,
    out_ref,
    halo_ref,
    mesh_w,
    mean_w,
    read_w,
    weights,
    enc_lo,
    enc_hi,
    enc_onehot,
    enc_pick,
    nbr_hi,
    nbr_lo,
    nbr_hit,
    bias_ref,
    dec_pick,
    latent_ref,
    query_ref,
    key_ref,
    value_ref,
    score_a,
    score_b,
    expo_a,
    expo_b,
    sum_ref,
    peak_ref,
    context_ref,
    local_sem,
    send_sem,
    recv_sem,
):
    lat = lax.axis_index("lat")
    lon = lax.axis_index("lon")
    parity = lax.rem(lon, 2)
    inner = lon + 1 - 2 * parity
    outer = lax.rem(lon + 2 * parity - 1 + SECTORS, SECTORS)
    core = (lat, inner)
    band = (1 - lat, lon)
    band_core = (1 - lat, inner)
    far = (1 - lat, outer)
    near = (lat, outer)

    loads = [
        pltpu.make_async_copy(source, weights.at[i], local_sem.at[i])
        for i, source in enumerate(
            (w_encode_hbm, w_key_hbm, w_value_hbm, w_query_hbm, w_output_hbm, w_decode_hbm)
        )
    ]
    own_load = pltpu.make_async_copy(mesh_ref, mesh_w.at[0], local_sem.at[6])

    barrier = pltpu.get_barrier_semaphore()
    for peer in (core, band, band_core, far, near):
        pl.semaphore_signal(barrier, inc=1, device_id=peer, device_id_type=MESH)
    pl.semaphore_wait(barrier, 5)

    number = iter(range(64))

    def remote(source, target, peer):
        i = next(number)
        return pltpu.make_async_remote_copy(
            src_ref=source,
            dst_ref=target,
            send_sem=send_sem.at[i],
            recv_sem=recv_sem.at[i],
            device_id=peer,
            device_id_type=MESH,
        )

    main = ROWS * COLS
    edge = ROWS * HALO
    inner_edge = pl.ds(pl.multiple_of(main + edge * (1 - parity), edge), edge)
    outer_edge = pl.ds(pl.multiple_of(main + edge * parity, edge), edge)

    def landing(i):
        return halo_ref.at[:, main + i * edge : main + (i + 1) * edge]

    grids = [
        remote(grid_ref.at[:, inner_edge], landing(0), core),
        remote(grid_ref.at[:, outer_edge], landing(1), near),
        remote(grid_ref.at[:, inner_edge], landing(2), band_core),
        remote(grid_ref.at[:, outer_edge], landing(3), far),
        remote(grid_ref.at[:, 0:main], halo_ref.at[:, 0:main], band),
    ]
    for copy in grids:
        copy.start()

    def piece(c):
        return pl.ds(c * CHUNK, CHUNK)

    to_far = [remote(mesh_ref.at[piece(c)], mesh_w.at[2, piece(c)], far) for c in (3, 0, 1, 2)]
    to_band = [remote(mesh_ref.at[piece(c)], mesh_w.at[3, piece(c)], band) for c in range(CHUNKS)]
    on_band = remote(mesh_w.at[2, piece(3)], mesh_w.at[5, piece(3)], band)
    on_far = [remote(mesh_w.at[3, piece(c)], mesh_w.at[5, piece(c)], far) for c in range(3)]
    means = [
        remote(mean_w.at[0], mean_w.at[slot], peer) for slot, peer in ((2, far), (3, band), (5, near))
    ]

    def slot_rows(slot):
        return pl.ds(slot * NB, NB)

    shares = [
        [
            remote(key_ref.at[slot_rows(slot)], key_ref.at[slot_rows(slot + 1)], core),
            remote(value_ref.at[:, slot_rows(slot)], value_ref.at[:, slot_rows(slot + 1)], core),
        ]
        for slot in (0, 3)
    ]
    reads = [
        remote(read_w.at[0], read_w.at[slot], peer)
        for slot, peer in ((1, core), (2, far), (3, band), (4, band_core), (5, near))
    ]
    for c in range(CHUNKS):
        to_far[c].start()
        to_band[c].start()
    own_load.start()
    for load in loads:
        load.start()

    build_enc(enc_src_ref[...], enc_count_ref[...], lat, parity, enc_lo, enc_hi, enc_onehot, enc_pick)
    build_mask(nbr_ref[...], nbr_count_ref[...], lat, lon, inner, nbr_hi, nbr_lo, nbr_hit, bias_ref)
    build_dec(dec_src_ref, lat, lon, inner, dec_pick)
    for h in range(HEADS):
        for first, last in ((0, 1), (2, 4), (5, 6)):
            value_ref[h * VROWS + HEAD : (h + 1) * VROWS, first * NB : last * NB] = jnp.ones(
                (VROWS - HEAD, (last - first) * NB), bf16
            )
    for copy in grids:
        copy.wait_recv()
    summed = (
        dot(grid_ref[:, 0:main], enc_pick[0:main, :])
        + dot(halo_ref[:, 0:main], enc_pick[main : 2 * main, :])
        + dot(halo_ref[:, main:], enc_pick[2 * main :, :])
    )
    mean_w[0] = (summed / enc_count_ref[...].astype(f32)).astype(bf16)
    for copy in means:
        copy.start()

    own_load.wait()
    for load in loads:
        load.wait()

    def phase_loop(phase, carry):
        def block(i, carry):
            step = 2 * phase + i

            @pl.when(step == 1)
            def _():
                to_far[0].wait_recv()
                on_band.start()
                to_band[0].wait_recv()
                on_far[0].start()
                means[0].wait_recv()
                for copy in to_far[1:]:
                    copy.wait_recv()
                for copy in shares[0]:
                    copy.start()

            @pl.when(step == 2)
            def _():
                means[1].wait_recv()
                to_band[3].wait_recv()

            @pl.when(step == 3)
            def _():
                means[2].wait_recv()
                on_band.wait_recv()
                for copy in on_far:
                    copy.wait_recv()
                for copy in shares[1]:
                    copy.start()

            slot = 3 * phase + 2 * i
            embedded = silu(
                lax.dot_general(
                    mean_w[slot], w_embed_ref[...], (((0,), (0,)), ((), ())), preferred_element_type=f32
                )
            ).astype(bf16)
            latent = mesh_w[slot].astype(f32) + dot(embedded, weights[0])
            normed = layer_norm(latent, gain_attn_ref[...]).astype(bf16)
            rows = pl.ds(pl.multiple_of(slot * NB, NB), NB)
            key_ref[rows, :] = dot(normed, weights[1]).astype(bf16)
            values = dot(normed, weights[2]).T.astype(bf16)
            for h in range(HEADS):
                value_ref[h * VROWS : h * VROWS + HEAD, rows] = values[h * HEAD : (h + 1) * HEAD, :]

            @pl.when(step == 0)
            def _():
                latent_ref[...] = latent
                query_ref[...] = (dot(normed, weights[3]).astype(bf16).astype(f32) * 0.125).astype(bf16)

            return carry

        lax.fori_loop(0, 2, block, 0)

        @pl.when(phase == 0)
        def _():
            to_band[1].wait_recv()
            on_far[1].start()
            for copy in shares[0]:
                copy.wait_recv()

        @pl.when(phase == 1)
        def _():
            for copy in shares[1]:
                copy.wait_recv()

        def midway(p):
            @pl.when(jnp.logical_and(phase == 0, p == HEADS // 4))
            def _():
                to_band[2].wait_recv()
                on_far[2].start()

        attention(
            phase,
            query_ref,
            key_ref,
            value_ref,
            bias_ref,
            (score_a, score_b),
            (expo_a, expo_b),
            sum_ref,
            peak_ref,
            midway,
        )
        return carry

    lax.fori_loop(0, 2, phase_loop, 0)

    def merge(h, carry):
        peak_a = peak_ref[0, pl.ds(h, 1), :]
        peak_b = peak_ref[1, pl.ds(h, 1), :]
        peak = jnp.maximum(peak_a, peak_b)
        joined = sum_ref[0, h] * jnp.exp(peak_a - peak) + sum_ref[1, h] * jnp.exp(peak_b - peak)
        context_ref[pl.ds(pl.multiple_of(h * HEAD, HEAD), HEAD), :] = (
            joined[0:HEAD, :] / joined[HEAD : HEAD + 1, :]
        ).astype(bf16)
        return carry

    lax.fori_loop(0, HEADS, merge, 0)
    mixed = latent_ref[...] + lax.dot_general(
        context_ref[...], weights[4], (((0,), (0,)), ((), ())), preferred_element_type=f32
    )
    normed_out = layer_norm(mixed, gain_dec_ref[...]).astype(bf16)
    decoded = silu(dot(normed_out, weights[5])).astype(bf16)
    read_w[0] = lax.dot_general(
        w_readout_ref[...], decoded, (((1,), (1,)), ((), ())), preferred_element_type=f32
    ).astype(bf16)
    for copy in reads:
        copy.start()

    def add_slots(slots, first, last):
        def chunk(c, carry):
            lanes = pl.ds(pl.multiple_of(c * NB, NB), NB)
            update = sum(dot(read_w[b], dec_pick[c, b * NB : (b + 1) * NB, :]) for b in slots)
            if not first:
                update = update + out_ref[:, lanes]
            if last:
                update = grid_ref[:, lanes].astype(f32) + update / 3.0
            out_ref[:, lanes] = update
            return carry

        lax.fori_loop(0, main // NB, chunk, 0)

    add_slots((0,), True, False)
    reads[0].wait_recv()
    add_slots((1,), False, False)
    for copy in reads[1:]:
        copy.wait_recv()
    add_slots((2, 3, 4, 5), False, True)
    for copy in grids + to_far + to_band + [on_band] + on_far + means + shares[0] + shares[1] + reads:
        copy.wait_send()


def body(
    grid_state,
    mesh_feat,
    enc_src,
    enc_count,
    nbr_ids,
    nbr_count,
    dec_src,
    w_embed,
    w_encode,
    w_query,
    w_key,
    w_value,
    w_output,
    w_decode,
    w_readout,
    norm_attn,
    norm_dec,
):
    main = ROWS * COLS
    packed = jnp.concatenate(
        [
            grid_state.reshape(V, main),
            grid_state[:, :, :HALO].reshape(V, ROWS * HALO),
            grid_state[:, :, COLS - HALO :].reshape(V, ROWS * HALO),
        ],
        axis=1,
    )
    vmem = pl.BlockSpec(memory_space=pltpu.VMEM)
    hbm = pl.BlockSpec(memory_space=pl.ANY)
    out = pl.pallas_call(
        kernel,
        out_shape=jax.ShapeDtypeStruct((V, main), f32),
        in_specs=[vmem, hbm] + [vmem] * 6 + [hbm] * 6 + [vmem] * 3,
        out_specs=vmem,
        scratch_shapes=[
            pltpu.VMEM((V, main + 4 * ROWS * HALO), bf16),
            pltpu.VMEM((SLOTS, NB, D), bf16),
            pltpu.VMEM((SLOTS, V, NB), bf16),
            pltpu.VMEM((SLOTS, V, NB), bf16),
            pltpu.VMEM((6, D, D), bf16),
            pltpu.VMEM((KE, NB), f32),
            pltpu.VMEM((KE, NB), f32),
            pltpu.VMEM((KE * COLS, NB), bf16),
            pltpu.VMEM((40 * COLS, NB), bf16),
            pltpu.VMEM((KM, NB), f32),
            pltpu.VMEM((KM, NB), f32),
            pltpu.VMEM((KM * SLOTS * 16, NB), bf16),
            pltpu.VMEM((WINDOW, NB), f32),
            pltpu.VMEM((8, WINDOW, NB), bf16),
            pltpu.VMEM((NB, D), f32),
            pltpu.VMEM((NB, D), bf16),
            pltpu.VMEM((WINDOW, D), bf16),
            pltpu.VMEM((HEADS * VROWS, WINDOW), bf16),
            pltpu.VMEM((HALF, NB), f32),
            pltpu.VMEM((HALF, NB), f32),
            pltpu.VMEM((HALF, NB), bf16),
            pltpu.VMEM((HALF, NB), bf16),
            pltpu.VMEM((2, HEADS, VROWS, NB), f32),
            pltpu.VMEM((2, HEADS, NB), f32),
            pltpu.VMEM((D, NB), bf16),
            pltpu.SemaphoreType.DMA((7,)),
            pltpu.SemaphoreType.DMA((64,)),
            pltpu.SemaphoreType.DMA((64,)),
        ],
        compiler_params=pltpu.CompilerParams(
            collective_id=0, has_side_effects=True, vmem_limit_bytes=64 * 1024 * 1024 - 65536
        ),
        name="denoise",
    )(
        packed,
        mesh_feat,
        enc_src,
        enc_count.reshape(1, NB),
        nbr_ids,
        nbr_count.reshape(1, NB),
        dec_src,
        w_embed,
        w_encode,
        w_query,
        w_key,
        w_value,
        w_output,
        w_decode,
        w_readout.T,
        norm_attn.reshape(1, D),
        norm_dec.reshape(1, D),
    )
    return out.reshape(V, ROWS, COLS)


def solution(mesh):
    in_specs = (
        P(None, "lat", "lon"),
        P(("lat", "lon"), None),
        P(None, ("lat", "lon")),
        P(("lat", "lon")),
        P(None, ("lat", "lon")),
        P(("lat", "lon")),
        P(None, "lat", "lon"),
    ) + (P(),) * 10
    return jax.shard_map(
        body, mesh=mesh, in_specs=in_specs, out_specs=P(None, "lat", "lon"), check_vma=False
    )
```

```python
import jax
import jax.numpy as jnp
from jax import lax
from jax.experimental import pallas as pl
from jax.experimental.pallas import tpu as pltpu
from jax.sharding import PartitionSpec as P

f32, bf16, i32 = jnp.float32, jnp.bfloat16, jnp.int32
MESH = pl.DeviceIdType.MESH
V = 84
D = 1024
NB = 256
KE = 16
KM = 32
ROWS = 16
COLS = 128
HALO = 16
SLOTS = 6
WINDOW = SLOTS * NB
SECTORS = 64
CHUNKS = 4
CHUNK = NB // CHUNKS
HEADS = 16
HEAD = 64
VROWS = 80
HALF = WINDOW // 2
NEG = -1e30


def tile16(row):
    return jnp.broadcast_to(row, (16, row.shape[1])).astype(bf16)


def rep(tile, times):
    return jnp.concatenate([tile] * times, axis=0)


def row_codes(rows, cols, base=0):
    return (lax.broadcasted_iota(i32, (rows, cols), 0) + base).astype(f32).astype(bf16)


def flag(mask):
    return jnp.where(mask, jnp.ones((), bf16), jnp.zeros((), bf16))


def slot_of(node, lat, lon, inner):
    member = (node & (NB - 1)).astype(f32)
    device = node >> 8
    far = (device >> 6) ^ lat
    sector = device & (SECTORS - 1)
    slot = jnp.where(sector == lon, 3 * far, jnp.where(sector == inner, 1 + 3 * far, 5 - 3 * far))
    return slot.astype(f32), member


def pack_grid(grid_ref, flat_ref, edge_ref):
    rows = jnp.transpose(grid_ref[...], (1, 0, 2))
    lane = lax.broadcasted_iota(i32, (1, COLS), 1)
    for r in range(ROWS):
        flat_ref[:, r * COLS : (r + 1) * COLS] = rows[r]
    for east in range(2):
        for half in range(2):
            strip = jnp.zeros((V, COLS), f32)
            for k in range(8):
                row = rows[half * 8 + k].astype(f32)
                turn = (k * HALO - (COLS - HALO) * east) % COLS
                row = pltpu.roll(row, turn, 1) if turn else row
                strip = jnp.where((lane >= k * HALO) & (lane < (k + 1) * HALO), row, strip)
            at = (2 * east + half) * COLS
            edge_ref[:, at : at + COLS] = strip.astype(bf16)


def build_enc(src, count, lat, parity, lo_ref, hi_ref, onehot_ref, a_ref):
    row = (src * 6554) >> 20
    place = src - row * (COLS + 2 * HALO)
    r = row & (ROWS - 1)
    west = place < HALO
    east = place >= HALO + COLS
    halo = west | east
    c = jnp.where(east, place - (HALO + COLS), place)
    side = jnp.where(east, 1, 0)
    outer = side ^ (1 - parity)
    hi = jnp.where(halo, 16 + 2 * outer + (r >> 3), r)
    lo = jnp.where(halo, (r & 7) * HALO + c, place - HALO)
    live = (lax.broadcasted_iota(i32, src.shape, 0) < count) & ((row >> 4) == lat)
    hi_ref[...] = jnp.where(live, hi, -1).astype(f32)
    lo_ref[...] = lo.astype(f32)
    iota = row_codes(COLS, NB)
    for s in range(KE):
        onehot_ref[s * COLS : (s + 1) * COLS, :] = flag(iota == rep(tile16(lo_ref[s : s + 1, :]), 8))

    def group(g, carry):
        code = g.astype(f32)
        acc = jnp.zeros((COLS, NB), bf16)
        for s in range(KE):
            hit = tile16(jnp.where(hi_ref[s : s + 1, :] == code, 1.0, 0.0))
            acc = acc + onehot_ref[s * COLS : (s + 1) * COLS, :] * rep(hit, 8)
        a_ref[pl.ds(pl.multiple_of(g * COLS, COLS), COLS), :] = acc
        return carry

    lax.fori_loop(0, 20, group, 0)


def build_mask(ids, count, lat, lon, inner, hi_ref, lo_ref, hit_ref, bias_ref):
    slot, member = slot_of(ids, lat, lon, inner)
    live = lax.broadcasted_iota(i32, ids.shape, 0) < count
    hi_ref[...] = jnp.where(live, slot, -1.0)
    lo_ref[...] = member
    for s in range(KM):
        for b in range(SLOTS):
            at = (s * SLOTS + b) * 16
            hit_ref[at : at + 16, :] = tile16(jnp.where(hi_ref[s : s + 1, :] == float(b), 1.0, 0.0))
    step = 32

    def chunk(c, carry):
        iota = row_codes(step, NB, c * step)
        acc = [jnp.zeros((step, NB), bf16) for _ in range(SLOTS)]
        for s in range(KM):
            one = flag(iota == rep(tile16(lo_ref[s : s + 1, :]), step // 16))
            for b in range(SLOTS):
                at = (s * SLOTS + b) * 16
                acc[b] = acc[b] + one * rep(hit_ref[at : at + 16, :], step // 16)
        for b in range(SLOTS):
            rows = pl.ds(pl.multiple_of(b * NB + c * step, step), step)
            bias_ref[rows, :] = jnp.where(acc[b].astype(f32) > 0.0, 0.0, NEG)
        return carry

    lax.fori_loop(0, NB // step, chunk, 0)


def build_dec(src_ref, lat, lon, inner, pick_ref):
    def chunk(c, carry):
        for half in range(2):
            lanes = slice(half * COLS, (half + 1) * COLS)
            codes = []
            for i in range(3):
                ids = src_ref[i, pl.ds(c * 2 + half, 1), :]
                slot, member = slot_of(ids, lat, lon, inner)
                hits = [tile16(jnp.where(slot == float(b), 1.0, 0.0)) for b in range(SLOTS)]
                codes.append((tile16(member), hits))
            for k in range(4):
                iota = row_codes(64, COLS, k * 64)
                ones = [flag(iota == rep(member, 4)) for member, _ in codes]
                for b in range(SLOTS):
                    at = b * NB + k * 64
                    pick_ref[c, at : at + 64, lanes] = (
                        ones[0] * rep(codes[0][1][b], 4)
                        + ones[1] * rep(codes[1][1][b], 4)
                        + ones[2] * rep(codes[2][1][b], 4)
                    )
        return carry

    lax.fori_loop(0, 8, chunk, 0)


def silu(u):
    return u * jax.nn.sigmoid(u)


def layer_norm(x, gain):
    centre = x - jnp.mean(x, axis=-1, keepdims=True)
    spread = jnp.mean(centre * centre, axis=-1, keepdims=True)
    return centre * lax.rsqrt(spread + 1e-05) * gain


def dot(a, b):
    return jnp.dot(a, b, preferred_element_type=f32)


def attention(part, q_ref, k_ref, v_ref, bias_ref, score_refs, expo_refs, sum_ref, peak_ref):
    low = lax.broadcasted_iota(i32, (1, 128), 1) < 64
    zero = jnp.zeros((), bf16)
    span = pl.ds(pl.multiple_of(part * HALF, HALF), HALF)

    def scores(p, half):
        cols = pl.ds(pl.multiple_of(p * 128, 128), 128)
        own = low if half == 0 else jnp.logical_not(low)
        score_refs[half][...] = lax.dot_general(
            k_ref[span, cols],
            jnp.where(own, q_ref[:, cols], zero),
            (((1,), (1,)), ((), ())),
            preferred_element_type=f32,
        )

    def weigh(h, half):
        masked = score_refs[half][...] + bias_ref[span, :]
        peak = jnp.max(masked, axis=0, keepdims=True)
        expo_refs[half][...] = jnp.exp(masked - peak).astype(bf16)
        peak_ref[part, pl.ds(h, 1), :] = peak

    def gather(h, half):
        rows = pl.ds(pl.multiple_of(h * VROWS, 16), VROWS)
        sum_ref[part, h] = dot(v_ref[rows, span], expo_refs[half][...])

    scores(0, 0)

    def pair(p, carry):
        scores(p, 1)
        gather(jnp.maximum(2 * p - 1, 0), 1)
        weigh(2 * p, 0)
        scores(jnp.minimum(p + 1, HEADS // 2 - 1), 0)
        gather(2 * p, 0)
        weigh(2 * p + 1, 1)
        return carry

    lax.fori_loop(0, HEADS // 2, pair, 0)
    gather(HEADS - 1, 1)


def kernel(
    grid_ref,
    mesh_ref,
    enc_src_ref,
    enc_count_ref,
    nbr_ref,
    nbr_count_ref,
    dec_src_ref,
    w_embed_ref,
    w_encode_hbm,
    w_query_hbm,
    w_key_hbm,
    w_value_hbm,
    w_output_hbm,
    w_decode_hbm,
    w_readout_ref,
    gain_attn_ref,
    gain_dec_ref,
    out_ref,
    flat_ref,
    edge_ref,
    halo_ref,
    peer_src,
    peer_count,
    part_out,
    part_in,
    total_ref,
    mesh_w,
    mean_w,
    read_w,
    weights,
    enc_lo,
    enc_hi,
    enc_onehot,
    enc_pick,
    peer_pick,
    nbr_hi,
    nbr_lo,
    nbr_hit,
    bias_ref,
    dec_pick,
    latent_ref,
    query_ref,
    key_ref,
    value_ref,
    score_a,
    score_b,
    expo_a,
    expo_b,
    sum_ref,
    peak_ref,
    context_ref,
    local_sem,
    send_sem,
    recv_sem,
):
    lat = lax.axis_index("lat")
    lon = lax.axis_index("lon")
    parity = lax.rem(lon, 2)
    inner = lon + 1 - 2 * parity
    outer = lax.rem(lon + 2 * parity - 1 + SECTORS, SECTORS)
    core = (lat, inner)
    band = (1 - lat, lon)
    band_core = (1 - lat, inner)
    far = (1 - lat, outer)
    near = (lat, outer)

    loads = [
        pltpu.make_async_copy(source, weights.at[i], local_sem.at[i])
        for i, source in enumerate(
            (w_encode_hbm, w_key_hbm, w_value_hbm, w_query_hbm, w_output_hbm, w_decode_hbm)
        )
    ]
    own_load = pltpu.make_async_copy(mesh_ref, mesh_w.at[0], local_sem.at[6])

    barrier = pltpu.get_barrier_semaphore()
    for peer in (core, band, band_core, far, near):
        pl.semaphore_signal(barrier, inc=1, device_id=peer, device_id_type=MESH)
    own_load.start()
    for load in loads:
        load.start()
    pack_grid(grid_ref, flat_ref, edge_ref)
    pl.semaphore_wait(barrier, 5)

    number = iter(range(64))

    def remote(source, target, peer):
        i = next(number)
        return pltpu.make_async_remote_copy(
            src_ref=source,
            dst_ref=target,
            send_sem=send_sem.at[i],
            recv_sem=recv_sem.at[i],
            device_id=peer,
            device_id_type=MESH,
        )

    main = ROWS * COLS
    edge = ROWS * HALO
    inner_edge = pl.ds(pl.multiple_of(edge * (1 - parity), edge), edge)
    outer_edge = pl.ds(pl.multiple_of(edge * parity, edge), edge)
    grids = [
        remote(enc_src_ref, peer_src, band),
        remote(enc_count_ref, peer_count, band),
        remote(edge_ref.at[:, inner_edge], halo_ref.at[:, 0:edge], core),
        remote(edge_ref.at[:, outer_edge], halo_ref.at[:, edge : 2 * edge], near),
    ]
    part = remote(part_out, part_in, band)
    for copy in grids:
        copy.start()

    def piece(c):
        return pl.ds(c * CHUNK, CHUNK)

    order = (2, 3, 0, 1)
    to_far = {c: remote(mesh_ref.at[piece(c)], mesh_w.at[2, piece(c)], far) for c in order}
    to_band = [remote(mesh_ref.at[piece(c)], mesh_w.at[3, piece(c)], band) for c in range(CHUNKS)]
    on_band = {c: remote(mesh_w.at[2, piece(c)], mesh_w.at[5, piece(c)], band) for c in (2, 3)}
    on_far = [remote(mesh_w.at[3, piece(c)], mesh_w.at[5, piece(c)], far) for c in range(2)]
    means = [
        remote(mean_w.at[0], mean_w.at[slot], peer) for slot, peer in ((2, far), (3, band), (5, near))
    ]

    def slot_rows(slot):
        return pl.ds(slot * NB, NB)

    shares = [
        [
            remote(key_ref.at[slot_rows(slot)], key_ref.at[slot_rows(slot + 1)], core),
            remote(value_ref.at[:, slot_rows(slot)], value_ref.at[:, slot_rows(slot + 1)], core),
        ]
        for slot in (0, 3)
    ]
    reads = [
        remote(read_w.at[0], read_w.at[slot], peer)
        for slot, peer in ((1, core), (2, far), (3, band), (4, band_core), (5, near))
    ]
    for c in order:
        to_far[c].start()
    to_band[0].start()

    build_enc(enc_src_ref[...], enc_count_ref[...], lat, parity, enc_lo, enc_hi, enc_onehot, enc_pick)
    for copy in grids[:2]:
        copy.wait_recv()
    build_enc(peer_src[...], peer_count[...], lat, parity, enc_lo, enc_hi, enc_onehot, peer_pick)
    for copy in grids[2:]:
        copy.wait_recv()
    part_out[...] = dot(flat_ref[...], peer_pick[0:main, :]) + dot(halo_ref[...], peer_pick[main:, :])
    summed = dot(flat_ref[...], enc_pick[0:main, :]) + dot(halo_ref[...], enc_pick[main:, :])
    part.start()
    for c in range(1, CHUNKS):
        to_band[c].start()
    to_far[2].wait_recv()
    on_band[2].start()
    to_band[0].wait_recv()
    on_far[0].start()
    for h in range(HEADS):
        for first, last in ((0, 1), (2, 4), (5, 6)):
            value_ref[h * VROWS + HEAD : (h + 1) * VROWS, first * NB : last * NB] = jnp.ones(
                (VROWS - HEAD, (last - first) * NB), bf16
            )
    build_dec(dec_src_ref, lat, lon, inner, dec_pick)
    part.wait_recv()
    mean_w[0] = ((summed + part_in[...]) / enc_count_ref[...].astype(f32)).astype(bf16)
    to_far[3].wait_recv()
    on_band[3].start()
    own_load.wait()
    for copy in means:
        copy.start()
    for load in loads[:4]:
        load.wait()

    def phase_loop(phase, carry):
        def block(i, carry):
            step = 2 * phase + i

            @pl.when(step == 1)
            def _():
                to_band[1].wait_recv()
                on_far[1].start()
                for copy in shares[0]:
                    copy.start()
                build_mask(nbr_ref[...], nbr_count_ref[...], lat, lon, inner, nbr_hi, nbr_lo, nbr_hit, bias_ref)
                to_far[0].wait_recv()
                to_far[1].wait_recv()
                means[0].wait_recv()

            @pl.when(step == 2)
            def _():
                means[1].wait_recv()
                to_band[2].wait_recv()
                to_band[3].wait_recv()

            @pl.when(step == 3)
            def _():
                for copy in shares[1]:
                    copy.start()
                means[2].wait_recv()
                for copy in (on_band[2], on_band[3], on_far[0], on_far[1]):
                    copy.wait_recv()

            slot = 3 * phase + 2 * i
            embedded = silu(
                lax.dot_general(
                    mean_w[slot], w_embed_ref[...], (((0,), (0,)), ((), ())), preferred_element_type=f32
                )
            ).astype(bf16)
            latent = mesh_w[slot].astype(f32) + dot(embedded, weights[0])
            normed = layer_norm(latent, gain_attn_ref[...]).astype(bf16)
            rows = pl.ds(pl.multiple_of(slot * NB, NB), NB)
            key_ref[rows, :] = dot(normed, weights[1]).astype(bf16)
            values = dot(normed, weights[2]).T.astype(bf16)
            for h in range(HEADS):
                value_ref[h * VROWS : h * VROWS + HEAD, rows] = values[h * HEAD : (h + 1) * HEAD, :]

            @pl.when(step == 0)
            def _():
                latent_ref[...] = latent
                query_ref[...] = (dot(normed, weights[3]).astype(bf16).astype(f32) * 0.125).astype(bf16)

            return carry

        lax.fori_loop(0, 2, block, 0)

        @pl.when(phase == 0)
        def _():
            for copy in shares[0]:
                copy.wait_recv()

        @pl.when(phase == 1)
        def _():
            for copy in shares[1]:
                copy.wait_recv()

        attention(
            phase,
            query_ref,
            key_ref,
            value_ref,
            bias_ref,
            (score_a, score_b),
            (expo_a, expo_b),
            sum_ref,
            peak_ref,
        )
        return carry

    lax.fori_loop(0, 2, phase_loop, 0)

    def merge(h, carry):
        peak_a = peak_ref[0, pl.ds(h, 1), :]
        peak_b = peak_ref[1, pl.ds(h, 1), :]
        peak = jnp.maximum(peak_a, peak_b)
        joined = sum_ref[0, h] * jnp.exp(peak_a - peak) + sum_ref[1, h] * jnp.exp(peak_b - peak)
        context_ref[pl.ds(pl.multiple_of(h * HEAD, HEAD), HEAD), :] = (
            joined[0:HEAD, :] / joined[HEAD : HEAD + 1, :]
        ).astype(bf16)
        return carry

    lax.fori_loop(0, HEADS, merge, 0)
    for load in loads[4:]:
        load.wait()
    mixed = latent_ref[...] + lax.dot_general(
        context_ref[...], weights[4], (((0,), (0,)), ((), ())), preferred_element_type=f32
    )
    normed_out = layer_norm(mixed, gain_dec_ref[...]).astype(bf16)
    decoded = silu(dot(normed_out, weights[5])).astype(bf16)
    read_w[0] = lax.dot_general(
        w_readout_ref[...], decoded, (((1,), (1,)), ((), ())), preferred_element_type=f32
    ).astype(bf16)
    for copy in reads:
        copy.start()

    def add_slots(slots, first, last):
        def chunk(c, carry):
            lanes = pl.ds(pl.multiple_of(c * NB, NB), NB)
            update = sum(dot(read_w[b], dec_pick[c, b * NB : (b + 1) * NB, :]) for b in slots)
            if not first:
                update = update + total_ref[:, lanes]
            if last:
                update = flat_ref[:, lanes].astype(f32) + update / 3.0
                out_ref[:, 2 * c, :] = update[:, :COLS]
                out_ref[:, 2 * c + 1, :] = update[:, COLS:]
            else:
                total_ref[:, lanes] = update
            return carry

        lax.fori_loop(0, main // NB, chunk, 0)

    add_slots((0,), True, False)
    reads[0].wait_recv()
    add_slots((1,), False, False)
    for copy in reads[1:]:
        copy.wait_recv()
    add_slots((2, 3, 4, 5), False, True)
    blocks = list(to_far.values()) + to_band + list(on_band.values()) + on_far
    for copy in grids + [part] + blocks + means + shares[0] + shares[1] + reads:
        copy.wait_send()


def body(
    grid_state,
    mesh_feat,
    enc_src,
    enc_count,
    nbr_ids,
    nbr_count,
    dec_src,
    w_embed,
    w_encode,
    w_query,
    w_key,
    w_value,
    w_output,
    w_decode,
    w_readout,
    norm_attn,
    norm_dec,
):
    main = ROWS * COLS
    vmem = pl.BlockSpec(memory_space=pltpu.VMEM)
    hbm = pl.BlockSpec(memory_space=pl.ANY)
    out = pl.pallas_call(
        kernel,
        out_shape=jax.ShapeDtypeStruct((V, ROWS, COLS), f32),
        in_specs=[vmem, hbm] + [vmem] * 6 + [hbm] * 6 + [vmem] * 3,
        out_specs=vmem,
        scratch_shapes=[
            pltpu.VMEM((V, main), bf16),
            pltpu.VMEM((V, 2 * ROWS * HALO), bf16),
            pltpu.VMEM((V, 2 * ROWS * HALO), bf16),
            pltpu.VMEM((KE, NB), i32),
            pltpu.VMEM((1, NB), i32),
            pltpu.VMEM((V, NB), f32),
            pltpu.VMEM((V, NB), f32),
            pltpu.VMEM((V, main), f32),
            pltpu.VMEM((SLOTS, NB, D), bf16),
            pltpu.VMEM((SLOTS, V, NB), bf16),
            pltpu.VMEM((SLOTS, V, NB), bf16),
            pltpu.VMEM((6, D, D), bf16),
            pltpu.VMEM((KE, NB), f32),
            pltpu.VMEM((KE, NB), f32),
            pltpu.VMEM((KE * COLS, NB), bf16),
            pltpu.VMEM((20 * COLS, NB), bf16),
            pltpu.VMEM((20 * COLS, NB), bf16),
            pltpu.VMEM((KM, NB), f32),
            pltpu.VMEM((KM, NB), f32),
            pltpu.VMEM((KM * SLOTS * 16, NB), bf16),
            pltpu.VMEM((WINDOW, NB), f32),
            pltpu.VMEM((8, WINDOW, NB), bf16),
            pltpu.VMEM((NB, D), f32),
            pltpu.VMEM((NB, D), bf16),
            pltpu.VMEM((WINDOW, D), bf16),
            pltpu.VMEM((HEADS * VROWS, WINDOW), bf16),
            pltpu.VMEM((HALF, NB), f32),
            pltpu.VMEM((HALF, NB), f32),
            pltpu.VMEM((HALF, NB), bf16),
            pltpu.VMEM((HALF, NB), bf16),
            pltpu.VMEM((2, HEADS, VROWS, NB), f32),
            pltpu.VMEM((2, HEADS, NB), f32),
            pltpu.VMEM((D, NB), bf16),
            pltpu.SemaphoreType.DMA((7,)),
            pltpu.SemaphoreType.DMA((64,)),
            pltpu.SemaphoreType.DMA((64,)),
        ],
        compiler_params=pltpu.CompilerParams(
            collective_id=0, has_side_effects=True, vmem_limit_bytes=64 * 1024 * 1024 - 65536
        ),
        name="denoise",
    )(
        grid_state,
        mesh_feat,
        enc_src,
        enc_count.reshape(1, NB),
        nbr_ids,
        nbr_count.reshape(1, NB),
        dec_src,
        w_embed,
        w_encode,
        w_query,
        w_key,
        w_value,
        w_output,
        w_decode,
        w_readout.T,
        norm_attn.reshape(1, D),
        norm_dec.reshape(1, D),
    )
    return out


def solution(mesh):
    in_specs = (
        P(None, "lat", "lon"),
        P(("lat", "lon"), None),
        P(None, ("lat", "lon")),
        P(("lat", "lon")),
        P(None, ("lat", "lon")),
        P(("lat", "lon")),
        P(None, "lat", "lon"),
    ) + (P(),) * 10
    return jax.shard_map(
        body, mesh=mesh, in_specs=in_specs, out_specs=P(None, "lat", "lon"), check_vma=False
    )
```

```python
import jax
import jax.numpy as jnp
from jax import lax
from jax.experimental import pallas as pl
from jax.experimental.pallas import tpu as pltpu
from jax.sharding import PartitionSpec as P

f32, bf16, i32 = jnp.float32, jnp.bfloat16, jnp.int32
MESH = pl.DeviceIdType.MESH
V = 84
D = 1024
NB = 256
KE = 16
KM = 32
ROWS = 16
COLS = 128
HALO = 16
SLOTS = 6
WINDOW = SLOTS * NB
SECTORS = 64
CHUNKS = 4
CHUNK = NB // CHUNKS
HEADS = 16
HEAD = 64
VROWS = 80
HB = NB // 2
HALF = WINDOW // 2
NEG = -1e30


def tile16(row):
    return jnp.broadcast_to(row, (16, row.shape[1])).astype(bf16)


def rep(tile, times):
    return jnp.concatenate([tile] * times, axis=0)


def row_codes(rows, cols, base=0):
    return (lax.broadcasted_iota(i32, (rows, cols), 0) + base).astype(f32).astype(bf16)


def flag(mask):
    return jnp.where(mask, jnp.ones((), bf16), jnp.zeros((), bf16))


def slot_of(node, lat, lon, inner):
    member = (node & (NB - 1)).astype(f32)
    device = node >> 8
    far = (device >> 6) ^ lat
    sector = device & (SECTORS - 1)
    slot = jnp.where(sector == lon, 3 * far, jnp.where(sector == inner, 1 + 3 * far, 5 - 3 * far))
    return slot.astype(f32), member


def pack_grid(grid_ref, flat_ref, edge_ref):
    rows = jnp.transpose(grid_ref[...], (1, 0, 2))
    lane = lax.broadcasted_iota(i32, (1, COLS), 1)
    for r in range(ROWS):
        flat_ref[:, r * COLS : (r + 1) * COLS] = rows[r]
    for east in range(2):
        for half in range(2):
            strip = jnp.zeros((V, COLS), f32)
            for k in range(8):
                row = rows[half * 8 + k].astype(f32)
                turn = (k * HALO - (COLS - HALO) * east) % COLS
                row = pltpu.roll(row, turn, 1) if turn else row
                strip = jnp.where((lane >= k * HALO) & (lane < (k + 1) * HALO), row, strip)
            at = (2 * east + half) * COLS
            edge_ref[:, at : at + COLS] = strip.astype(bf16)


def build_enc(src, count, lat, parity, lo_ref, hi_ref, onehot_ref, a_ref):
    row = (src * 6554) >> 20
    place = src - row * (COLS + 2 * HALO)
    r = row & (ROWS - 1)
    west = place < HALO
    east = place >= HALO + COLS
    halo = west | east
    c = jnp.where(east, place - (HALO + COLS), place)
    side = jnp.where(east, 1, 0)
    outer = side ^ (1 - parity)
    hi = jnp.where(halo, 16 + 2 * outer + (r >> 3), r)
    lo = jnp.where(halo, (r & 7) * HALO + c, place - HALO)
    live = (lax.broadcasted_iota(i32, src.shape, 0) < count) & ((row >> 4) == lat)
    hi_ref[...] = jnp.where(live, hi, -1).astype(f32)
    lo_ref[...] = lo.astype(f32)
    iota = row_codes(COLS, NB)
    for s in range(KE):
        onehot_ref[s * COLS : (s + 1) * COLS, :] = flag(iota == rep(tile16(lo_ref[s : s + 1, :]), 8))

    def group(g, carry):
        code = g.astype(f32)
        acc = jnp.zeros((COLS, NB), bf16)
        for s in range(KE):
            hit = tile16(jnp.where(hi_ref[s : s + 1, :] == code, 1.0, 0.0))
            acc = acc + onehot_ref[s * COLS : (s + 1) * COLS, :] * rep(hit, 8)
        a_ref[pl.ds(pl.multiple_of(g * COLS, COLS), COLS), :] = acc
        return carry

    lax.fori_loop(0, 20, group, 0)


def build_mask(ids, count, lat, lon, inner, hi_ref, lo_ref, hit_ref, bias_ref):
    slot, member = slot_of(ids, lat, lon, inner)
    live = lax.broadcasted_iota(i32, ids.shape, 0) < count
    hi_ref[...] = jnp.where(live, slot, -1.0)
    lo_ref[...] = member
    for s in range(KM):
        for b in range(SLOTS):
            at = (s * SLOTS + b) * 16
            hit_ref[at : at + 16, :] = tile16(jnp.where(hi_ref[s : s + 1, :] == float(b), 1.0, 0.0))
    step = 32

    def chunk(c, carry):
        iota = row_codes(step, NB, c * step)
        acc = [jnp.zeros((step, NB), bf16) for _ in range(SLOTS)]
        for s in range(KM):
            one = flag(iota == rep(tile16(lo_ref[s : s + 1, :]), step // 16))
            for b in range(SLOTS):
                at = (s * SLOTS + b) * 16
                acc[b] = acc[b] + one * rep(hit_ref[at : at + 16, :], step // 16)
        for b in range(SLOTS):
            shift = jnp.where(c < NB // step // 2, 0, HB)
            start = (0, NB, 2 * NB + shift, 3 * NB + HB - 3 * shift, 4 * NB, 5 * NB)[b]
            rows = pl.ds(pl.multiple_of(start + c * step, step), step)
            bias_ref[rows, :] = jnp.where(acc[b].astype(f32) > 0.0, 0.0, NEG)
        return carry

    lax.fori_loop(0, NB // step, chunk, 0)


def build_dec(src_ref, lat, lon, inner, pick_ref):
    def chunk(c, carry):
        for half in range(2):
            lanes = slice(half * COLS, (half + 1) * COLS)
            codes = []
            for i in range(3):
                ids = src_ref[i, pl.ds(c * 2 + half, 1), :]
                slot, member = slot_of(ids, lat, lon, inner)
                hits = [tile16(jnp.where(slot == float(b), 1.0, 0.0)) for b in range(SLOTS)]
                codes.append((tile16(member), hits))
            for k in range(4):
                iota = row_codes(64, COLS, k * 64)
                ones = [flag(iota == rep(member, 4)) for member, _ in codes]
                for b in range(SLOTS):
                    at = b * NB + k * 64
                    pick_ref[c, at : at + 64, lanes] = (
                        ones[0] * rep(codes[0][1][b], 4)
                        + ones[1] * rep(codes[1][1][b], 4)
                        + ones[2] * rep(codes[2][1][b], 4)
                    )
        return carry

    lax.fori_loop(0, 8, chunk, 0)


def silu(u):
    return u * jax.nn.sigmoid(u)


def layer_norm(x, gain):
    centre = x - jnp.mean(x, axis=-1, keepdims=True)
    spread = jnp.mean(centre * centre, axis=-1, keepdims=True)
    return centre * lax.rsqrt(spread + 1e-05) * gain


def dot(a, b):
    return jnp.dot(a, b, preferred_element_type=f32)


def attention(part, q_ref, k_ref, v_ref, bias_ref, score_refs, expo_refs, sum_ref, peak_ref):
    low = lax.broadcasted_iota(i32, (1, 128), 1) < 64
    zero = jnp.zeros((), bf16)
    span = pl.ds(pl.multiple_of(part * HALF, HALF), HALF)

    def scores(p, half):
        cols = pl.ds(pl.multiple_of(p * 128, 128), 128)
        own = low if half == 0 else jnp.logical_not(low)
        score_refs[half][...] = lax.dot_general(
            k_ref[span, cols],
            jnp.where(own, q_ref[:, cols], zero),
            (((1,), (1,)), ((), ())),
            preferred_element_type=f32,
        )

    def weigh(h, half):
        masked = score_refs[half][...] + bias_ref[span, :]
        peak = jnp.max(masked, axis=0, keepdims=True)
        expo_refs[half][...] = jnp.exp(masked - peak).astype(bf16)
        peak_ref[part, pl.ds(h, 1), :] = peak

    def gather(h, half):
        rows = pl.ds(pl.multiple_of(h * VROWS, 16), VROWS)
        sum_ref[part, h] = dot(v_ref[rows, span], expo_refs[half][...])

    scores(0, 0)

    def pair(p, carry):
        scores(p, 1)
        gather(jnp.maximum(2 * p - 1, 0), 1)
        weigh(2 * p, 0)
        scores(jnp.minimum(p + 1, HEADS // 2 - 1), 0)
        gather(2 * p, 0)
        weigh(2 * p + 1, 1)
        return carry

    lax.fori_loop(0, HEADS // 2, pair, 0)
    gather(HEADS - 1, 1)


def kernel(
    grid_ref,
    mesh_ref,
    enc_src_ref,
    enc_count_ref,
    nbr_ref,
    nbr_count_ref,
    dec_src_ref,
    w_embed_ref,
    w_encode_hbm,
    w_query_hbm,
    w_key_hbm,
    w_value_hbm,
    w_output_hbm,
    w_decode_hbm,
    w_readout_ref,
    gain_attn_ref,
    gain_dec_ref,
    out_ref,
    flat_ref,
    edge_ref,
    halo_ref,
    peer_src,
    peer_count,
    part_out,
    part_in,
    total_ref,
    mesh_w,
    mean_w,
    read_w,
    weights,
    enc_lo,
    enc_hi,
    enc_onehot,
    enc_pick,
    peer_pick,
    nbr_hi,
    nbr_lo,
    nbr_hit,
    bias_ref,
    dec_pick,
    latent_ref,
    query_ref,
    key_ref,
    value_ref,
    score_a,
    score_b,
    expo_a,
    expo_b,
    sum_ref,
    peak_ref,
    context_ref,
    local_sem,
    send_sem,
    recv_sem,
):
    lat = lax.axis_index("lat")
    lon = lax.axis_index("lon")
    parity = lax.rem(lon, 2)
    inner = lon + 1 - 2 * parity
    outer = lax.rem(lon + 2 * parity - 1 + SECTORS, SECTORS)
    core = (lat, inner)
    band = (1 - lat, lon)
    band_core = (1 - lat, inner)
    far = (1 - lat, outer)
    near = (lat, outer)

    loads = [
        pltpu.make_async_copy(source, weights.at[i], local_sem.at[i])
        for i, source in enumerate(
            (w_encode_hbm, w_key_hbm, w_value_hbm, w_query_hbm, w_output_hbm, w_decode_hbm)
        )
    ]
    own_load = pltpu.make_async_copy(mesh_ref, mesh_w.at[0], local_sem.at[6])

    barrier = pltpu.get_barrier_semaphore()
    for peer in (core, band, band_core, far, near):
        pl.semaphore_signal(barrier, inc=1, device_id=peer, device_id_type=MESH)
    own_load.start()
    for load in loads:
        load.start()
    pack_grid(grid_ref, flat_ref, edge_ref)
    pl.semaphore_wait(barrier, 5)

    number = iter(range(64))

    def remote(source, target, peer):
        i = next(number)
        return pltpu.make_async_remote_copy(
            src_ref=source,
            dst_ref=target,
            send_sem=send_sem.at[i],
            recv_sem=recv_sem.at[i],
            device_id=peer,
            device_id_type=MESH,
        )

    main = ROWS * COLS
    edge = ROWS * HALO
    inner_edge = pl.ds(pl.multiple_of(edge * (1 - parity), edge), edge)
    outer_edge = pl.ds(pl.multiple_of(edge * parity, edge), edge)
    grids = [
        remote(enc_src_ref, peer_src, band),
        remote(enc_count_ref, peer_count, band),
        remote(edge_ref.at[:, inner_edge], halo_ref.at[:, 0:edge], core),
        remote(edge_ref.at[:, outer_edge], halo_ref.at[:, edge : 2 * edge], near),
    ]
    part = remote(part_out, part_in, band)
    for copy in grids:
        copy.start()

    def piece(c):
        return pl.ds(c * CHUNK, CHUNK)

    def place(unit, half, c):
        return mesh_w.at[unit, pl.ds(half * HB + c % 2 * CHUNK, CHUNK)]

    order = (2, 3, 0, 1)
    to_far = [remote(mesh_ref.at[piece(c)], place(1 + c // 2, 0, c), far) for c in range(CHUNKS)]
    to_band = {c: remote(mesh_ref.at[piece(c)], place(2 - c // 2, 1, c), band) for c in order}
    on_band = [remote(place(1, 0, c), place(3, 0, c), band) for c in (0, 1)]
    on_far = [remote(place(1, 1, c), place(3, 1, c), far) for c in (2, 3)]
    means = [
        remote(mean_w.at[0], mean_w.at[2], far),
        remote(mean_w.at[1], mean_w.at[3], band),
        remote(mean_w.at[1], mean_w.at[4], far),
        remote(mean_w.at[0], mean_w.at[5], band),
        remote(mean_w.at[0:2], mean_w.at[6:8], near),
    ]

    def share(start, size, target):
        source, target = pl.ds(start, size), pl.ds(target, size)
        return [
            remote(key_ref.at[source], key_ref.at[target], core),
            remote(value_ref.at[:, source], value_ref.at[:, target], core),
        ]

    shares = [
        share(0, NB, NB),
        share(2 * NB + HB, HB, 4 * NB + HB),
        share(3 * NB + HB, HB, 4 * NB),
    ]
    reads = [
        remote(read_w.at[0], read_w.at[slot], peer)
        for slot, peer in ((1, core), (2, far), (3, band), (4, band_core), (5, near))
    ]
    for c in (0, 1):
        to_far[c].start()
    to_band[2].start()

    build_enc(enc_src_ref[...], enc_count_ref[...], lat, parity, enc_lo, enc_hi, enc_onehot, enc_pick)
    for copy in grids[:2]:
        copy.wait_recv()
    build_enc(peer_src[...], peer_count[...], lat, parity, enc_lo, enc_hi, enc_onehot, peer_pick)
    summed = dot(flat_ref[...], enc_pick[0:main, :])
    for copy in grids[2:]:
        copy.wait_recv()
    part_out[...] = dot(flat_ref[...], peer_pick[0:main, :]) + dot(halo_ref[...], peer_pick[main:, :])
    summed = summed + dot(halo_ref[...], enc_pick[main:, :])
    part.start()
    to_band[3].start()
    to_band[2].wait_recv()
    on_far[0].start()
    for h in range(HEADS):
        for first, last in ((0, 1), (2, 4), (5, 6)):
            value_ref[h * VROWS + HEAD : (h + 1) * VROWS, first * NB : last * NB] = jnp.ones(
                (VROWS - HEAD, (last - first) * NB), bf16
            )
    build_mask(nbr_ref[...], nbr_count_ref[...], lat, lon, inner, nbr_hi, nbr_lo, nbr_hit, bias_ref)
    part.wait_recv()
    mean = ((summed + part_in[...]) / enc_count_ref[...].astype(f32)).astype(bf16)
    mean_w[0] = mean[:, :HB]
    mean_w[1] = mean[:, HB:]
    own_load.wait()
    for copy in means:
        copy.start()
    for c in (0, 1):
        to_far[c + 2].start()
        to_band[c].start()
    for c in (0, 1):
        to_far[c].wait_recv()
        on_band[c].start()
    for load in loads[:4]:
        load.wait()

    def phase_loop(phase, carry):
        def block(i, carry):
            step = 2 * phase + i

            @pl.when(step == 1)
            def _():
                to_band[3].wait_recv()
                on_far[1].start()
                for copy in means[:2]:
                    copy.wait_recv()
                for copy in shares[0]:
                    copy.start()

            @pl.when(step == 2)
            def _():
                for copy in means[2:4] + [to_far[2], to_far[3], to_band[0], to_band[1]]:
                    copy.wait_recv()
                for copy in shares[1]:
                    copy.start()

            @pl.when(step == 3)
            def _():
                for copy in means[4:] + on_band + on_far:
                    copy.wait_recv()
                for copy in shares[2]:
                    copy.start()

            unit_mean = jnp.concatenate([mean_w[2 * step], mean_w[2 * step + 1]], axis=1)
            embedded = silu(
                lax.dot_general(
                    unit_mean, w_embed_ref[...], (((0,), (0,)), ((), ())), preferred_element_type=f32
                )
            ).astype(bf16)
            latent = mesh_w[step].astype(f32) + dot(embedded, weights[0])
            normed = layer_norm(latent, gain_attn_ref[...]).astype(bf16)
            rows = pl.ds(pl.multiple_of(jnp.where(step == 3, 5, step + jnp.minimum(step, 1)) * NB, NB), NB)
            key_ref[rows, :] = dot(normed, weights[1]).astype(bf16)
            values = dot(normed, weights[2]).T.astype(bf16)
            for h in range(HEADS):
                value_ref[h * VROWS : h * VROWS + HEAD, rows] = values[h * HEAD : (h + 1) * HEAD, :]

            @pl.when(step == 0)
            def _():
                latent_ref[...] = latent
                query_ref[...] = (dot(normed, weights[3]).astype(bf16).astype(f32) * 0.125).astype(bf16)

            return carry

        lax.fori_loop(0, 2, block, 0)

        @pl.when(phase == 0)
        def _():
            for copy in shares[0]:
                copy.wait_recv()

        @pl.when(phase == 1)
        def _():
            for copy in shares[1] + shares[2]:
                copy.wait_recv()

        attention(
            phase,
            query_ref,
            key_ref,
            value_ref,
            bias_ref,
            (score_a, score_b),
            (expo_a, expo_b),
            sum_ref,
            peak_ref,
        )
        return carry

    lax.fori_loop(0, 2, phase_loop, 0)

    def merge(h, carry):
        peak_a = peak_ref[0, pl.ds(h, 1), :]
        peak_b = peak_ref[1, pl.ds(h, 1), :]
        peak = jnp.maximum(peak_a, peak_b)
        joined = sum_ref[0, h] * jnp.exp(peak_a - peak) + sum_ref[1, h] * jnp.exp(peak_b - peak)
        context_ref[pl.ds(pl.multiple_of(h * HEAD, HEAD), HEAD), :] = (
            joined[0:HEAD, :] / joined[HEAD : HEAD + 1, :]
        ).astype(bf16)
        return carry

    lax.fori_loop(0, HEADS, merge, 0)
    for load in loads[4:]:
        load.wait()
    mixed = latent_ref[...] + lax.dot_general(
        context_ref[...], weights[4], (((0,), (0,)), ((), ())), preferred_element_type=f32
    )
    normed_out = layer_norm(mixed, gain_dec_ref[...]).astype(bf16)
    decoded = silu(dot(normed_out, weights[5])).astype(bf16)
    read_w[0] = lax.dot_general(
        w_readout_ref[...], decoded, (((1,), (1,)), ((), ())), preferred_element_type=f32
    ).astype(bf16)
    for copy in reads:
        copy.start()
    build_dec(dec_src_ref, lat, lon, inner, dec_pick)

    def add_slots(slots, first, last):
        def chunk(c, carry):
            lanes = pl.ds(pl.multiple_of(c * NB, NB), NB)
            update = sum(dot(read_w[b], dec_pick[c, b * NB : (b + 1) * NB, :]) for b in slots)
            if not first:
                update = update + total_ref[:, lanes]
            if last:
                update = flat_ref[:, lanes].astype(f32) + update / 3.0
                out_ref[:, 2 * c, :] = update[:, :COLS]
                out_ref[:, 2 * c + 1, :] = update[:, COLS:]
            else:
                total_ref[:, lanes] = update
            return carry

        lax.fori_loop(0, main // NB, chunk, 0)

    add_slots((0,), True, False)
    reads[0].wait_recv()
    add_slots((1,), False, False)
    for copy in reads[1:]:
        copy.wait_recv()
    add_slots((2, 3, 4, 5), False, True)
    blocks = to_far + list(to_band.values()) + on_band + on_far
    for copy in grids + [part] + blocks + means + shares[0] + shares[1] + shares[2] + reads:
        copy.wait_send()


def body(
    grid_state,
    mesh_feat,
    enc_src,
    enc_count,
    nbr_ids,
    nbr_count,
    dec_src,
    w_embed,
    w_encode,
    w_query,
    w_key,
    w_value,
    w_output,
    w_decode,
    w_readout,
    norm_attn,
    norm_dec,
):
    main = ROWS * COLS
    vmem = pl.BlockSpec(memory_space=pltpu.VMEM)
    hbm = pl.BlockSpec(memory_space=pl.ANY)
    out = pl.pallas_call(
        kernel,
        out_shape=jax.ShapeDtypeStruct((V, ROWS, COLS), f32),
        in_specs=[vmem, hbm] + [vmem] * 6 + [hbm] * 6 + [vmem] * 3,
        out_specs=vmem,
        scratch_shapes=[
            pltpu.VMEM((V, main), bf16),
            pltpu.VMEM((V, 2 * ROWS * HALO), bf16),
            pltpu.VMEM((V, 2 * ROWS * HALO), bf16),
            pltpu.VMEM((KE, NB), i32),
            pltpu.VMEM((1, NB), i32),
            pltpu.VMEM((V, NB), f32),
            pltpu.VMEM((V, NB), f32),
            pltpu.VMEM((V, main), f32),
            pltpu.VMEM((4, NB, D), bf16),
            pltpu.VMEM((8, V, HB), bf16),
            pltpu.VMEM((SLOTS, V, NB), bf16),
            pltpu.VMEM((6, D, D), bf16),
            pltpu.VMEM((KE, NB), f32),
            pltpu.VMEM((KE, NB), f32),
            pltpu.VMEM((KE * COLS, NB), bf16),
            pltpu.VMEM((20 * COLS, NB), bf16),
            pltpu.VMEM((20 * COLS, NB), bf16),
            pltpu.VMEM((KM, NB), f32),
            pltpu.VMEM((KM, NB), f32),
            pltpu.VMEM((KM * SLOTS * 16, NB), bf16),
            pltpu.VMEM((WINDOW, NB), f32),
            pltpu.VMEM((8, WINDOW, NB), bf16),
            pltpu.VMEM((NB, D), f32),
            pltpu.VMEM((NB, D), bf16),
            pltpu.VMEM((WINDOW, D), bf16),
            pltpu.VMEM((HEADS * VROWS, WINDOW), bf16),
            pltpu.VMEM((HALF, NB), f32),
            pltpu.VMEM((HALF, NB), f32),
            pltpu.VMEM((HALF, NB), bf16),
            pltpu.VMEM((HALF, NB), bf16),
            pltpu.VMEM((2, HEADS, VROWS, NB), f32),
            pltpu.VMEM((2, HEADS, NB), f32),
            pltpu.VMEM((D, NB), bf16),
            pltpu.SemaphoreType.DMA((7,)),
            pltpu.SemaphoreType.DMA((64,)),
            pltpu.SemaphoreType.DMA((64,)),
        ],
        compiler_params=pltpu.CompilerParams(
            collective_id=0, has_side_effects=True, vmem_limit_bytes=64 * 1024 * 1024 - 65536
        ),
        name="denoise",
    )(
        grid_state,
        mesh_feat,
        enc_src,
        enc_count.reshape(1, NB),
        nbr_ids,
        nbr_count.reshape(1, NB),
        dec_src,
        w_embed,
        w_encode,
        w_query,
        w_key,
        w_value,
        w_output,
        w_decode,
        w_readout.T,
        norm_attn.reshape(1, D),
        norm_dec.reshape(1, D),
    )
    return out


def solution(mesh):
    in_specs = (
        P(None, "lat", "lon"),
        P(("lat", "lon"), None),
        P(None, ("lat", "lon")),
        P(("lat", "lon")),
        P(None, ("lat", "lon")),
        P(("lat", "lon")),
        P(None, "lat", "lon"),
    ) + (P(),) * 10
    return jax.shard_map(
        body, mesh=mesh, in_specs=in_specs, out_specs=P(None, "lat", "lon"), check_vma=False
    )
```

```python
import jax
import jax.numpy as jnp
from jax import lax
from jax.experimental import pallas as pl
from jax.experimental.pallas import tpu as pltpu
from jax.sharding import PartitionSpec as P

f32, bf16, i32 = jnp.float32, jnp.bfloat16, jnp.int32
MESH = pl.DeviceIdType.MESH
V = 84
D = 1024
NB = 256
KE = 16
KM = 32
ROWS = 16
COLS = 128
HALO = 16
SLOTS = 6
WINDOW = SLOTS * NB
SECTORS = 64
CHUNKS = 4
CHUNK = NB // CHUNKS
HEADS = 16
HEAD = 64
VROWS = 80
HB = NB // 2
HALF = WINDOW // 2
NEG = -1e30
VMEM_BYTES = 64 * 1024 * 1024 - 65536 - V * ROWS * COLS * 4 - 8192


def tile16(row):
    return jnp.broadcast_to(row, (16, row.shape[1])).astype(bf16)


def rep(tile, times):
    return jnp.concatenate([tile] * times, axis=0)


def row_codes(rows, cols, base=0):
    return (lax.broadcasted_iota(i32, (rows, cols), 0) + base).astype(f32).astype(bf16)


def flag(mask):
    return jnp.where(mask, jnp.ones((), bf16), jnp.zeros((), bf16))


def slot_of(node, lat, lon, inner):
    member = node & (NB - 1)
    device = node >> 8
    far = (device >> 6) ^ lat
    sector = device & (SECTORS - 1)
    slot = jnp.where(sector == lon, 3 * far, jnp.where(sector == inner, 1 + 3 * far, 5 - 3 * far))
    return slot, member


def pack_grid(grid_ref, flat_ref, edge_ref):
    rows = jnp.transpose(grid_ref[...], (1, 0, 2))
    lane = lax.broadcasted_iota(i32, (1, COLS), 1)
    for r in range(ROWS):
        flat_ref[:, r * COLS : (r + 1) * COLS] = rows[r]
    for east in range(2):
        for half in range(2):
            strip = jnp.zeros((V, COLS), f32)
            for k in range(8):
                row = rows[half * 8 + k].astype(f32)
                turn = (k * HALO - (COLS - HALO) * east) % COLS
                row = pltpu.roll(row, turn, 1) if turn else row
                strip = jnp.where((lane >= k * HALO) & (lane < (k + 1) * HALO), row, strip)
            at = (2 * east + half) * COLS
            edge_ref[:, at : at + COLS] = strip.astype(bf16)


def build_enc(src, count, lat, parity, lo_ref, hi_ref, onehot_ref, a_ref):
    row = (src * 6554) >> 20
    place = src - row * (COLS + 2 * HALO)
    r = row & (ROWS - 1)
    west = place < HALO
    east = place >= HALO + COLS
    halo = west | east
    c = jnp.where(east, place - (HALO + COLS), place)
    side = jnp.where(east, 1, 0)
    outer = side ^ (1 - parity)
    hi = jnp.where(halo, 16 + 2 * outer + (r >> 3), r)
    lo = jnp.where(halo, (r & 7) * HALO + c, place - HALO)
    live = (lax.broadcasted_iota(i32, src.shape, 0) < count) & ((row >> 4) == lat)
    hi_ref[...] = jnp.where(live, hi, -1)
    lo_ref[...] = lo
    sub = lax.broadcasted_iota(i32, (16, NB), 0)
    for s in range(KE):
        at = jnp.broadcast_to(lo_ref[s : s + 1, :], (16, NB))
        onehot_ref[s * 16 : (s + 1) * 16, :] = jnp.where((at & 15) == sub, 1 << (4 * (at >> 4)), 0)

    def group(g, carry):
        halves = []
        for first in (0, KE // 2):
            acc = jnp.zeros((16, NB), i32)
            for s in range(first, first + KE // 2):
                hit = jnp.broadcast_to(hi_ref[s : s + 1, :], (16, NB)) == g
                acc = acc + jnp.where(hit, onehot_ref[s * 16 : (s + 1) * 16, :], 0)
            halves.append(acc)
        even = (halves[0] & 0x0F0F0F0F) + (halves[1] & 0x0F0F0F0F)
        odd = ((halves[0] >> 4) & 0x0F0F0F0F) + ((halves[1] >> 4) & 0x0F0F0F0F)
        for k in range(8):
            counts = ((odd if k % 2 else even) >> (8 * (k // 2))) & 0xFF
            rows = pl.ds(pl.multiple_of(g * COLS + k * 16, 16), 16)
            a_ref[rows, :] = counts.astype(f32).astype(bf16)
        return carry

    lax.fori_loop(0, 20, group, 0)


def build_mask(ids, count, lat, lon, inner, hi_ref, lo_ref, bias_ref):
    slot, member = slot_of(ids, lat, lon, inner)
    live = lax.broadcasted_iota(i32, ids.shape, 0) < count
    hi_ref[...] = jnp.where(live, slot, -1)
    lo_ref[...] = member
    sub = lax.broadcasted_iota(i32, (8, NB), 0)
    words = [jnp.zeros((8, NB), i32) for _ in range(SLOTS)]
    for s in range(KM):
        at = jnp.broadcast_to(lo_ref[s : s + 1, :], (8, NB))
        where = jnp.broadcast_to(hi_ref[s : s + 1, :], (8, NB))
        bit = jnp.where((at & 7) == sub, 1 << (at >> 3), 0)
        for b in range(SLOTS):
            words[b] = words[b] | jnp.where(where == b, bit, 0)
    for b in range(SLOTS):
        for k in range(32):
            late = k >= 16
            start = (0, NB, 2 * NB + HB * late, 3 * NB + HB - 3 * HB * late, 4 * NB, 5 * NB)[b]
            seen = (words[b] >> k) & 1
            bias_ref[start + 8 * k : start + 8 * k + 8, :] = jnp.where(seen == 1, 0.0, NEG)


def build_dec(src_ref, lat, lon, inner, pick_ref):
    def chunk(c, carry):
        for half in range(2):
            lanes = slice(half * COLS, (half + 1) * COLS)
            codes = []
            for i in range(3):
                ids = src_ref[i, pl.ds(c * 2 + half, 1), :]
                slot, member = slot_of(ids, lat, lon, inner)
                hits = [tile16(jnp.where(slot == b, 1.0, 0.0)) for b in range(SLOTS)]
                codes.append((tile16(member.astype(f32)), hits))
            for k in range(4):
                iota = row_codes(64, COLS, k * 64)
                ones = [flag(iota == rep(member, 4)) for member, _ in codes]
                for b in range(SLOTS):
                    at = b * NB + k * 64
                    pick_ref[c, at : at + 64, lanes] = (
                        ones[0] * rep(codes[0][1][b], 4)
                        + ones[1] * rep(codes[1][1][b], 4)
                        + ones[2] * rep(codes[2][1][b], 4)
                    )
        return carry

    lax.fori_loop(0, 8, chunk, 0)


def silu(u):
    return u * jax.nn.sigmoid(u)


def layer_norm(x, gain):
    centre = x - jnp.mean(x, axis=-1, keepdims=True)
    spread = jnp.mean(centre * centre, axis=-1, keepdims=True)
    return centre * lax.rsqrt(spread + 1e-05) * gain


def dot(a, b):
    return jnp.dot(a, b, preferred_element_type=f32)


def attention(part, q_ref, k_ref, v_ref, bias_ref, score_refs, expo_refs, sum_ref, peak_ref):
    low = lax.broadcasted_iota(i32, (1, 128), 1) < 64
    zero = jnp.zeros((), bf16)
    span = pl.ds(pl.multiple_of(part * HALF, HALF), HALF)

    def scores(p, half):
        cols = pl.ds(pl.multiple_of(p * 128, 128), 128)
        own = low if half == 0 else jnp.logical_not(low)
        score_refs[half][...] = lax.dot_general(
            k_ref[span, cols],
            jnp.where(own, q_ref[:, cols], zero),
            (((1,), (1,)), ((), ())),
            preferred_element_type=f32,
        )

    def weigh(h, half):
        masked = score_refs[half][...] + bias_ref[span, :]
        peak = jnp.max(masked, axis=0, keepdims=True)
        expo_refs[half][...] = jnp.exp(masked - peak).astype(bf16)
        peak_ref[part, pl.ds(h, 1), :] = peak

    def gather(h, half):
        rows = pl.ds(pl.multiple_of(h * VROWS, 16), VROWS)
        sum_ref[part, h] = dot(v_ref[rows, span], expo_refs[half][...])

    scores(0, 0)

    def pair(p, carry):
        scores(p, 1)
        gather(jnp.maximum(2 * p - 1, 0), 1)
        weigh(2 * p, 0)
        scores(jnp.minimum(p + 1, HEADS // 2 - 1), 0)
        gather(2 * p, 0)
        weigh(2 * p + 1, 1)
        return carry

    lax.fori_loop(0, HEADS // 2, pair, 0)
    gather(HEADS - 1, 1)


def kernel(
    grid_hbm,
    mesh_ref,
    enc_src_hbm,
    enc_count_hbm,
    nbr_hbm,
    nbr_count_hbm,
    dec_src_hbm,
    w_embed_hbm,
    w_encode_hbm,
    w_query_hbm,
    w_key_hbm,
    w_value_hbm,
    w_output_hbm,
    w_decode_hbm,
    w_readout_hbm,
    gain_attn_hbm,
    gain_dec_hbm,
    out_ref,
    grid_ref,
    enc_src_ref,
    enc_count_ref,
    nbr_ref,
    nbr_count_ref,
    dec_src_ref,
    w_embed_ref,
    w_readout_ref,
    gain_attn_ref,
    gain_dec_ref,
    flat_ref,
    edge_ref,
    halo_ref,
    peer_src,
    peer_count,
    part_out,
    part_in,
    total_ref,
    mesh_w,
    mean_w,
    read_w,
    weights,
    enc_lo,
    enc_hi,
    enc_onehot,
    enc_pick,
    peer_pick,
    nbr_hi,
    nbr_lo,
    bias_ref,
    dec_pick,
    latent_ref,
    query_ref,
    key_ref,
    value_ref,
    score_a,
    score_b,
    expo_a,
    expo_b,
    sum_ref,
    peak_ref,
    context_ref,
    local_sem,
    send_sem,
    recv_sem,
):
    lat = lax.axis_index("lat")
    lon = lax.axis_index("lon")
    parity = lax.rem(lon, 2)
    inner = lon + 1 - 2 * parity
    outer = lax.rem(lon + 2 * parity - 1 + SECTORS, SECTORS)
    core = (lat, inner)
    band = (1 - lat, lon)
    band_core = (1 - lat, inner)
    far = (1 - lat, outer)
    near = (lat, outer)

    loads = [
        pltpu.make_async_copy(source, weights.at[i], local_sem.at[i])
        for i, source in enumerate(
            (w_encode_hbm, w_key_hbm, w_value_hbm, w_query_hbm, w_output_hbm, w_decode_hbm)
        )
    ]
    own_load = pltpu.make_async_copy(mesh_ref, mesh_w.at[0], local_sem.at[6])

    pairs = (
        (grid_hbm, grid_ref),
        (enc_src_hbm, enc_src_ref),
        (enc_count_hbm, enc_count_ref),
        (nbr_hbm, nbr_ref),
        (nbr_count_hbm, nbr_count_ref),
        (dec_src_hbm, dec_src_ref),
        (w_embed_hbm, w_embed_ref),
        (gain_attn_hbm, gain_attn_ref),
        (w_readout_hbm, w_readout_ref),
        (gain_dec_hbm, gain_dec_ref),
    )
    smalls = [
        pltpu.make_async_copy(source, target, local_sem.at[7 + i])
        for i, (source, target) in enumerate(pairs)
    ]
    for copy in smalls:
        copy.start()

    barrier = pltpu.get_barrier_semaphore()
    for peer in (core, band, band_core, far, near):
        pl.semaphore_signal(barrier, inc=1, device_id=peer, device_id_type=MESH)
    own_load.start()
    for load in loads[:4]:
        load.start()
    smalls[0].wait()
    pack_grid(grid_ref, flat_ref, edge_ref)
    pl.semaphore_wait(barrier, 5)

    number = iter(range(64))

    def remote(source, target, peer):
        i = next(number)
        return pltpu.make_async_remote_copy(
            src_ref=source,
            dst_ref=target,
            send_sem=send_sem.at[i],
            recv_sem=recv_sem.at[i],
            device_id=peer,
            device_id_type=MESH,
        )

    main = ROWS * COLS
    edge = ROWS * HALO
    inner_edge = pl.ds(pl.multiple_of(edge * (1 - parity), edge), edge)
    outer_edge = pl.ds(pl.multiple_of(edge * parity, edge), edge)
    grids = [
        remote(enc_src_hbm, peer_src, band),
        remote(enc_count_hbm, peer_count, band),
        remote(edge_ref.at[:, inner_edge], halo_ref.at[:, 0:edge], core),
        remote(edge_ref.at[:, outer_edge], halo_ref.at[:, edge : 2 * edge], near),
    ]
    part = remote(part_out, part_in, band)
    for copy in grids:
        copy.start()

    def piece(c):
        return pl.ds(c * CHUNK, CHUNK)

    def place(unit, half, c):
        return mesh_w.at[unit, pl.ds(half * HB + c % 2 * CHUNK, CHUNK)]

    order = (2, 3, 0, 1)
    to_far = [remote(mesh_ref.at[piece(c)], place(1 + c // 2, 0, c), far) for c in range(CHUNKS)]
    to_band = {c: remote(mesh_ref.at[piece(c)], place(2 - c // 2, 1, c), band) for c in order}
    on_band = [remote(place(1, 0, c), place(3, 0, c), band) for c in (0, 1)]
    on_far = [remote(place(1, 1, c), place(3, 1, c), far) for c in (2, 3)]
    means = [
        remote(mean_w.at[0], mean_w.at[2], far),
        remote(mean_w.at[1], mean_w.at[3], band),
        remote(mean_w.at[1], mean_w.at[4], far),
        remote(mean_w.at[0], mean_w.at[5], band),
        remote(mean_w.at[0:2], mean_w.at[6:8], near),
    ]

    def share(start, size, target):
        source, target = pl.ds(start, size), pl.ds(target, size)
        return [
            remote(key_ref.at[source], key_ref.at[target], core),
            remote(value_ref.at[:, source], value_ref.at[:, target], core),
        ]

    shares = [
        share(0, NB, NB),
        share(2 * NB + HB, HB, 4 * NB + HB),
        share(3 * NB + HB, HB, 4 * NB),
    ]
    reads = [
        remote(read_w.at[0], read_w.at[slot], peer)
        for slot, peer in ((1, core), (2, far), (3, band), (4, band_core), (5, near))
    ]
    for c in (0, 1):
        to_far[c].start()
    to_band[2].start()

    for copy in smalls[1:3]:
        copy.wait()
    build_enc(enc_src_ref[...], enc_count_ref[...], lat, parity, enc_lo, enc_hi, enc_onehot, enc_pick)
    for copy in grids[:2]:
        copy.wait_recv()
    build_enc(peer_src[...], peer_count[...], lat, parity, enc_lo, enc_hi, enc_onehot, peer_pick)
    summed = dot(flat_ref[...], enc_pick[0:main, :])
    for copy in grids[2:]:
        copy.wait_recv()
    part_out[...] = dot(flat_ref[...], peer_pick[0:main, :]) + dot(halo_ref[...], peer_pick[main:, :])
    summed = summed + dot(halo_ref[...], enc_pick[main:, :])
    part.start()
    to_band[3].start()
    to_band[2].wait_recv()
    on_far[0].start()
    for h in range(HEADS):
        for first, last in ((0, 1), (2, 4), (5, 6)):
            value_ref[h * VROWS + HEAD : (h + 1) * VROWS, first * NB : last * NB] = jnp.ones(
                (VROWS - HEAD, (last - first) * NB), bf16
            )
    for copy in smalls[3:8]:
        copy.wait()
    build_mask(nbr_ref[...], nbr_count_ref[...], lat, lon, inner, nbr_hi, nbr_lo, bias_ref)
    build_dec(dec_src_ref, lat, lon, inner, dec_pick)
    part.wait_recv()
    mean = ((summed + part_in[...]) / enc_count_ref[...].astype(f32)).astype(bf16)
    mean_w[0] = mean[:, :HB]
    mean_w[1] = mean[:, HB:]
    own_load.wait()
    for copy in means:
        copy.start()
    for c in (0, 1):
        to_far[c + 2].start()
        to_band[c].start()
    for c in (0, 1):
        to_far[c].wait_recv()
        on_band[c].start()
    for load in loads[:3]:
        load.wait()
    for load in loads[4:]:
        load.start()

    def phase_loop(phase, carry):
        def block(i, carry):
            step = 2 * phase + i

            @pl.when(step == 1)
            def _():
                to_band[3].wait_recv()
                on_far[1].start()
                for copy in means[:2]:
                    copy.wait_recv()
                for copy in shares[0]:
                    copy.start()

            @pl.when(step == 2)
            def _():
                for copy in means[2:4] + [to_far[2], to_far[3], to_band[0], to_band[1]]:
                    copy.wait_recv()
                for copy in shares[1]:
                    copy.start()

            @pl.when(step == 3)
            def _():
                for copy in means[4:] + on_band + on_far:
                    copy.wait_recv()
                for copy in shares[2]:
                    copy.start()

            unit_mean = jnp.concatenate([mean_w[2 * step], mean_w[2 * step + 1]], axis=1)
            embedded = silu(
                lax.dot_general(
                    unit_mean, w_embed_ref[...], (((0,), (0,)), ((), ())), preferred_element_type=f32
                )
            ).astype(bf16)
            latent = mesh_w[step].astype(f32) + dot(embedded, weights[0])
            normed = layer_norm(latent, gain_attn_ref[...]).astype(bf16)
            rows = pl.ds(pl.multiple_of(jnp.where(step == 3, 5, step + jnp.minimum(step, 1)) * NB, NB), NB)
            key_ref[rows, :] = dot(normed, weights[1]).astype(bf16)
            values = dot(normed, weights[2]).T.astype(bf16)
            for h in range(HEADS):
                value_ref[h * VROWS : h * VROWS + HEAD, rows] = values[h * HEAD : (h + 1) * HEAD, :]

            @pl.when(step == 0)
            def _():
                latent_ref[...] = latent
                loads[3].wait()
                query_ref[...] = (dot(normed, weights[3]).astype(bf16).astype(f32) * 0.125).astype(bf16)

            return carry

        lax.fori_loop(0, 2, block, 0)

        @pl.when(phase == 0)
        def _():
            for copy in shares[0]:
                copy.wait_recv()

        @pl.when(phase == 1)
        def _():
            for copy in shares[1] + shares[2]:
                copy.wait_recv()

        attention(
            phase,
            query_ref,
            key_ref,
            value_ref,
            bias_ref,
            (score_a, score_b),
            (expo_a, expo_b),
            sum_ref,
            peak_ref,
        )
        return carry

    lax.fori_loop(0, 2, phase_loop, 0)

    def merge(h, carry):
        peak_a = peak_ref[0, pl.ds(h, 1), :]
        peak_b = peak_ref[1, pl.ds(h, 1), :]
        peak = jnp.maximum(peak_a, peak_b)
        joined = sum_ref[0, h] * jnp.exp(peak_a - peak) + sum_ref[1, h] * jnp.exp(peak_b - peak)
        context_ref[pl.ds(pl.multiple_of(h * HEAD, HEAD), HEAD), :] = (
            joined[0:HEAD, :] / joined[HEAD : HEAD + 1, :]
        ).astype(bf16)
        return carry

    lax.fori_loop(0, HEADS, merge, 0)
    for load in loads[4:] + smalls[8:]:
        load.wait()
    mixed = latent_ref[...] + lax.dot_general(
        context_ref[...], weights[4], (((0,), (0,)), ((), ())), preferred_element_type=f32
    )
    normed_out = layer_norm(mixed, gain_dec_ref[...]).astype(bf16)
    decoded = silu(dot(normed_out, weights[5])).astype(bf16)
    read_w[0] = lax.dot_general(
        w_readout_ref[...], decoded, (((1,), (1,)), ((), ())), preferred_element_type=f32
    ).astype(bf16)
    for copy in reads:
        copy.start()

    def add_slots(slots, first, last):
        def chunk(c, carry):
            lanes = pl.ds(pl.multiple_of(c * NB, NB), NB)
            update = sum(dot(read_w[b], dec_pick[c, b * NB : (b + 1) * NB, :]) for b in slots)
            if not first:
                update = update + total_ref[:, lanes]
            if last:
                update = flat_ref[:, lanes].astype(f32) + update / 3.0
                out_ref[:, 2 * c, :] = update[:, :COLS]
                out_ref[:, 2 * c + 1, :] = update[:, COLS:]
            else:
                total_ref[:, lanes] = update
            return carry

        lax.fori_loop(0, main // NB, chunk, 0)

    add_slots((0,), True, False)
    reads[0].wait_recv()
    add_slots((1,), False, False)
    for copy in reads[1:]:
        copy.wait_recv()
    add_slots((2, 3, 4, 5), False, True)
    blocks = to_far + list(to_band.values()) + on_band + on_far
    for copy in grids + [part] + blocks + means + shares[0] + shares[1] + shares[2] + reads:
        copy.wait_send()


def body(
    grid_state,
    mesh_feat,
    enc_src,
    enc_count,
    nbr_ids,
    nbr_count,
    dec_src,
    w_embed,
    w_encode,
    w_query,
    w_key,
    w_value,
    w_output,
    w_decode,
    w_readout,
    norm_attn,
    norm_dec,
):
    main = ROWS * COLS
    vmem = pl.BlockSpec(memory_space=pltpu.VMEM)
    hbm = pl.BlockSpec(memory_space=pl.ANY)
    out = pl.pallas_call(
        kernel,
        out_shape=pltpu.VMEM((V, ROWS, COLS), f32),
        in_specs=[hbm] * 17,
        out_specs=vmem,
        scratch_shapes=[
            pltpu.VMEM((V, ROWS, COLS), bf16),
            pltpu.VMEM((KE, NB), i32),
            pltpu.VMEM((1, NB), i32),
            pltpu.VMEM((KM, NB), i32),
            pltpu.VMEM((1, NB), i32),
            pltpu.VMEM((3, ROWS, COLS), i32),
            pltpu.VMEM((V, D), bf16),
            pltpu.VMEM((V, D), bf16),
            pltpu.VMEM((1, D), f32),
            pltpu.VMEM((1, D), f32),
            pltpu.VMEM((V, main), bf16),
            pltpu.VMEM((V, 2 * ROWS * HALO), bf16),
            pltpu.VMEM((V, 2 * ROWS * HALO), bf16),
            pltpu.VMEM((KE, NB), i32),
            pltpu.VMEM((1, NB), i32),
            pltpu.VMEM((V, NB), f32),
            pltpu.VMEM((V, NB), f32),
            pltpu.VMEM((V, main), f32),
            pltpu.VMEM((4, NB, D), bf16),
            pltpu.VMEM((8, V, HB), bf16),
            pltpu.VMEM((SLOTS, V, NB), bf16),
            pltpu.VMEM((6, D, D), bf16),
            pltpu.VMEM((KE, NB), i32),
            pltpu.VMEM((KE, NB), i32),
            pltpu.VMEM((KE * 16, NB), i32),
            pltpu.VMEM((20 * COLS, NB), bf16),
            pltpu.VMEM((20 * COLS, NB), bf16),
            pltpu.VMEM((KM, NB), i32),
            pltpu.VMEM((KM, NB), i32),
            pltpu.VMEM((WINDOW, NB), f32),
            pltpu.VMEM((8, WINDOW, NB), bf16),
            pltpu.VMEM((NB, D), f32),
            pltpu.VMEM((NB, D), bf16),
            pltpu.VMEM((WINDOW, D), bf16),
            pltpu.VMEM((HEADS * VROWS, WINDOW), bf16),
            pltpu.VMEM((HALF, NB), f32),
            pltpu.VMEM((HALF, NB), f32),
            pltpu.VMEM((HALF, NB), bf16),
            pltpu.VMEM((HALF, NB), bf16),
            pltpu.VMEM((2, HEADS, VROWS, NB), f32),
            pltpu.VMEM((2, HEADS, NB), f32),
            pltpu.VMEM((D, NB), bf16),
            pltpu.SemaphoreType.DMA((17,)),
            pltpu.SemaphoreType.DMA((64,)),
            pltpu.SemaphoreType.DMA((64,)),
        ],
        compiler_params=pltpu.CompilerParams(
            collective_id=0, has_side_effects=True, vmem_limit_bytes=VMEM_BYTES
        ),
        name="denoise",
    )(
        grid_state,
        mesh_feat,
        enc_src,
        enc_count.reshape(1, NB),
        nbr_ids,
        nbr_count.reshape(1, NB),
        dec_src,
        w_embed,
        w_encode,
        w_query,
        w_key,
        w_value,
        w_output,
        w_decode,
        w_readout.T,
        norm_attn.reshape(1, D),
        norm_dec.reshape(1, D),
    )
    return out


def solution(mesh):
    in_specs = (
        P(None, "lat", "lon"),
        P(("lat", "lon"), None),
        P(None, ("lat", "lon")),
        P(("lat", "lon")),
        P(None, ("lat", "lon")),
        P(("lat", "lon")),
        P(None, "lat", "lon"),
    ) + (P(),) * 10
    return jax.shard_map(
        body, mesh=mesh, in_specs=in_specs, out_specs=P(None, "lat", "lon"), check_vma=False
    )
```

```python
import jax
import jax.numpy as jnp
from jax import lax
from jax.experimental import pallas as pl
from jax.experimental.pallas import tpu as pltpu
from jax.sharding import PartitionSpec as P

f32, bf16, i32 = jnp.float32, jnp.bfloat16, jnp.int32
MESH = pl.DeviceIdType.MESH
V = 84
D = 1024
NB = 256
KE = 16
KM = 32
ROWS = 16
COLS = 128
HALO = 16
SLOTS = 6
WINDOW = SLOTS * NB
SECTORS = 64
CHUNKS = 4
CHUNK = NB // CHUNKS
HEADS = 16
HEAD = 64
VROWS = 80
HB = NB // 2
HALF = WINDOW // 2
NEG = -1e30
VMEM_BYTES = 64 * 1024 * 1024 - 65536 - V * ROWS * COLS * 4 - 8192


def tile16(row):
    return jnp.broadcast_to(row, (16, row.shape[1])).astype(bf16)


def rep(tile, times):
    return jnp.concatenate([tile] * times, axis=0)


def row_codes(rows, cols, base=0):
    return (lax.broadcasted_iota(i32, (rows, cols), 0) + base).astype(f32).astype(bf16)


def flag(mask):
    return jnp.where(mask, jnp.ones((), bf16), jnp.zeros((), bf16))


def slot_of(node, lat, lon, inner):
    member = node & (NB - 1)
    device = node >> 8
    far = (device >> 6) ^ lat
    sector = device & (SECTORS - 1)
    slot = jnp.where(sector == lon, 3 * far, jnp.where(sector == inner, 1 + 3 * far, 5 - 3 * far))
    return slot, member


def pack_grid(grid_ref, flat_ref, edge_ref):
    rows = jnp.transpose(grid_ref[...], (1, 0, 2))
    lane = lax.broadcasted_iota(i32, (1, COLS), 1)
    for r in range(ROWS):
        flat_ref[:, r * COLS : (r + 1) * COLS] = rows[r]
    for east in range(2):
        for half in range(2):
            strip = jnp.zeros((V, COLS), f32)
            for k in range(8):
                row = rows[half * 8 + k].astype(f32)
                turn = (k * HALO - (COLS - HALO) * east) % COLS
                row = pltpu.roll(row, turn, 1) if turn else row
                strip = jnp.where((lane >= k * HALO) & (lane < (k + 1) * HALO), row, strip)
            at = (2 * east + half) * COLS
            edge_ref[:, at : at + COLS] = strip.astype(bf16)


def build_enc(src, count, lat, parity, lo_ref, hi_ref, onehot_ref, a_ref):
    row = (src * 6554) >> 20
    place = src - row * (COLS + 2 * HALO)
    r = row & (ROWS - 1)
    west = place < HALO
    east = place >= HALO + COLS
    halo = west | east
    c = jnp.where(east, place - (HALO + COLS), place)
    side = jnp.where(east, 1, 0)
    outer = side ^ (1 - parity)
    hi = jnp.where(halo, 16 + 2 * outer + (r >> 3), r)
    lo = jnp.where(halo, (r & 7) * HALO + c, place - HALO)
    live = (lax.broadcasted_iota(i32, src.shape, 0) < count) & ((row >> 4) == lat)
    hi_ref[...] = jnp.where(live, hi, -1)
    lo_ref[...] = lo
    sub = lax.broadcasted_iota(i32, (16, NB), 0)
    for s in range(KE):
        at = jnp.broadcast_to(lo_ref[s : s + 1, :], (16, NB))
        onehot_ref[s * 16 : (s + 1) * 16, :] = jnp.where((at & 15) == sub, 1 << (4 * (at >> 4)), 0)

    def group(g, carry):
        halves = []
        for first in (0, KE // 2):
            acc = jnp.zeros((16, NB), i32)
            for s in range(first, first + KE // 2):
                hit = jnp.broadcast_to(hi_ref[s : s + 1, :], (16, NB)) == g
                acc = acc + jnp.where(hit, onehot_ref[s * 16 : (s + 1) * 16, :], 0)
            halves.append(acc)
        even = (halves[0] & 0x0F0F0F0F) + (halves[1] & 0x0F0F0F0F)
        odd = ((halves[0] >> 4) & 0x0F0F0F0F) + ((halves[1] >> 4) & 0x0F0F0F0F)
        for k in range(8):
            counts = ((odd if k % 2 else even) >> (8 * (k // 2))) & 0xFF
            rows = pl.ds(pl.multiple_of(g * COLS + k * 16, 16), 16)
            a_ref[rows, :] = counts.astype(f32).astype(bf16)
        return carry

    lax.fori_loop(0, 20, group, 0)


def build_mask(ids, count, lat, lon, inner, hi_ref, lo_ref, bias_ref):
    slot, member = slot_of(ids, lat, lon, inner)
    live = lax.broadcasted_iota(i32, ids.shape, 0) < count
    hi_ref[...] = jnp.where(live, slot, -1)
    lo_ref[...] = member
    sub = lax.broadcasted_iota(i32, (8, NB), 0)
    words = [jnp.zeros((8, NB), i32) for _ in range(SLOTS)]
    for s in range(KM):
        at = jnp.broadcast_to(lo_ref[s : s + 1, :], (8, NB))
        where = jnp.broadcast_to(hi_ref[s : s + 1, :], (8, NB))
        bit = jnp.where((at & 7) == sub, 1 << (at >> 3), 0)
        for b in range(SLOTS):
            words[b] = words[b] | jnp.where(where == b, bit, 0)
    for b in range(SLOTS):
        for k in range(32):
            late = k >= 16
            start = (0, NB, 2 * NB + HB * late, 3 * NB + HB - 3 * HB * late, 4 * NB, 5 * NB)[b]
            seen = (words[b] >> k) & 1
            bias_ref[start + 8 * k : start + 8 * k + 8, :] = jnp.where(seen == 1, 0.0, NEG)


def build_dec(src_ref, lat, lon, inner, pick_ref):
    def chunk(c, carry):
        for half in range(2):
            lanes = slice(half * COLS, (half + 1) * COLS)
            codes = []
            for i in range(3):
                ids = src_ref[i, pl.ds(c * 2 + half, 1), :]
                slot, member = slot_of(ids, lat, lon, inner)
                hits = [tile16(jnp.where(slot == b, 1.0, 0.0)) for b in range(SLOTS)]
                codes.append((tile16(member.astype(f32)), hits))
            for k in range(4):
                iota = row_codes(64, COLS, k * 64)
                ones = [flag(iota == rep(member, 4)) for member, _ in codes]
                for b in range(SLOTS):
                    at = b * NB + k * 64
                    pick_ref[c, at : at + 64, lanes] = (
                        ones[0] * rep(codes[0][1][b], 4)
                        + ones[1] * rep(codes[1][1][b], 4)
                        + ones[2] * rep(codes[2][1][b], 4)
                    )
        return carry

    lax.fori_loop(0, 8, chunk, 0)


def silu(u):
    return u * jax.nn.sigmoid(u)


def layer_norm(x, gain):
    centre = x - jnp.mean(x, axis=-1, keepdims=True)
    spread = jnp.mean(centre * centre, axis=-1, keepdims=True)
    return centre * lax.rsqrt(spread + 1e-05) * gain


def dot(a, b):
    return jnp.dot(a, b, preferred_element_type=f32)


def attention(part, q_ref, k_ref, v_ref, bias_ref, score_refs, expo_refs, sum_ref, peak_ref):
    low = lax.broadcasted_iota(i32, (1, 128), 1) < 64
    zero = jnp.zeros((), bf16)
    span = pl.ds(pl.multiple_of(part * HALF, HALF), HALF)

    def scores(p, half):
        cols = pl.ds(pl.multiple_of(p * 128, 128), 128)
        own = low if half == 0 else jnp.logical_not(low)
        score_refs[half][...] = lax.dot_general(
            k_ref[span, cols],
            jnp.where(own, q_ref[:, cols], zero),
            (((1,), (1,)), ((), ())),
            preferred_element_type=f32,
        )

    def weigh(h, half):
        masked = score_refs[half][...] + bias_ref[span, :]
        peak = jnp.max(masked, axis=0, keepdims=True)
        expo_refs[half][...] = jnp.exp(masked - peak).astype(bf16)
        peak_ref[part, pl.ds(h, 1), :] = peak

    def gather(h, half):
        rows = pl.ds(pl.multiple_of(h * VROWS, 16), VROWS)
        sum_ref[part, h] = dot(v_ref[rows, span], expo_refs[half][...])

    scores(0, 0)

    def pair(p, carry):
        scores(p, 1)
        gather(jnp.maximum(2 * p - 1, 0), 1)
        weigh(2 * p, 0)
        scores(jnp.minimum(p + 1, HEADS // 2 - 1), 0)
        gather(2 * p, 0)
        weigh(2 * p + 1, 1)
        return carry

    lax.fori_loop(0, HEADS // 2, pair, 0)
    gather(HEADS - 1, 1)


def kernel(
    grid_hbm,
    mesh_ref,
    enc_src_hbm,
    enc_count_hbm,
    nbr_hbm,
    nbr_count_hbm,
    dec_src_hbm,
    w_embed_hbm,
    w_encode_hbm,
    w_query_hbm,
    w_key_hbm,
    w_value_hbm,
    w_output_hbm,
    w_decode_hbm,
    w_readout_hbm,
    gain_attn_hbm,
    gain_dec_hbm,
    out_ref,
    grid_ref,
    enc_src_ref,
    enc_count_ref,
    nbr_ref,
    nbr_count_ref,
    dec_src_ref,
    w_embed_ref,
    w_readout_ref,
    gain_attn_ref,
    gain_dec_ref,
    flat_ref,
    edge_ref,
    halo_ref,
    peer_src,
    peer_count,
    part_out,
    part_in,
    total_ref,
    mesh_w,
    mean_w,
    read_w,
    weights,
    enc_lo,
    enc_hi,
    enc_onehot,
    enc_pick,
    peer_pick,
    nbr_hi,
    nbr_lo,
    bias_ref,
    dec_pick,
    latent_ref,
    query_ref,
    key_ref,
    value_ref,
    score_a,
    score_b,
    expo_a,
    expo_b,
    sum_ref,
    peak_ref,
    context_ref,
    local_sem,
    send_sem,
    recv_sem,
):
    lat = lax.axis_index("lat")
    lon = lax.axis_index("lon")
    parity = lax.rem(lon, 2)
    inner = lon + 1 - 2 * parity
    outer = lax.rem(lon + 2 * parity - 1 + SECTORS, SECTORS)
    core = (lat, inner)
    band = (1 - lat, lon)
    band_core = (1 - lat, inner)
    far = (1 - lat, outer)
    near = (lat, outer)

    loads = [
        pltpu.make_async_copy(source, weights.at[i], local_sem.at[i])
        for i, source in enumerate(
            (w_encode_hbm, w_key_hbm, w_value_hbm, w_query_hbm, w_output_hbm, w_decode_hbm)
        )
    ]
    own_load = pltpu.make_async_copy(mesh_ref, mesh_w.at[0], local_sem.at[6])

    pairs = (
        (grid_hbm, grid_ref),
        (enc_src_hbm, enc_src_ref),
        (enc_count_hbm, enc_count_ref),
        (nbr_hbm, nbr_ref),
        (nbr_count_hbm, nbr_count_ref),
        (dec_src_hbm, dec_src_ref),
        (w_embed_hbm, w_embed_ref),
        (gain_attn_hbm, gain_attn_ref),
        (w_readout_hbm, w_readout_ref),
        (gain_dec_hbm, gain_dec_ref),
    )
    smalls = [
        pltpu.make_async_copy(source, target, local_sem.at[7 + i])
        for i, (source, target) in enumerate(pairs)
    ]
    for copy in smalls:
        copy.start()

    barrier = pltpu.get_barrier_semaphore()
    for peer in (core, band, band_core, far, near):
        pl.semaphore_signal(barrier, inc=1, device_id=peer, device_id_type=MESH)
    own_load.start()
    for load in loads[:4]:
        load.start()
    smalls[0].wait()
    pack_grid(grid_ref, flat_ref, edge_ref)
    pl.semaphore_wait(barrier, 5)

    number = iter(range(64))

    def remote(source, target, peer):
        i = next(number)
        return pltpu.make_async_remote_copy(
            src_ref=source,
            dst_ref=target,
            send_sem=send_sem.at[i],
            recv_sem=recv_sem.at[i],
            device_id=peer,
            device_id_type=MESH,
        )

    main = ROWS * COLS
    edge = ROWS * HALO
    inner_edge = pl.ds(pl.multiple_of(edge * (1 - parity), edge), edge)
    outer_edge = pl.ds(pl.multiple_of(edge * parity, edge), edge)
    grids = [
        remote(enc_src_hbm, peer_src, band),
        remote(enc_count_hbm, peer_count, band),
        remote(edge_ref.at[:, inner_edge], halo_ref.at[:, 0:edge], core),
        remote(edge_ref.at[:, outer_edge], halo_ref.at[:, edge : 2 * edge], near),
    ]
    part = remote(part_out, part_in, band)
    for copy in grids:
        copy.start()

    def piece(c):
        return pl.ds(c * CHUNK, CHUNK)

    def place(unit, half, c):
        return mesh_w.at[unit, pl.ds(half * HB + c % 2 * CHUNK, CHUNK)]

    order = (2, 3, 0, 1)
    to_far = [remote(mesh_ref.at[piece(c)], place(1 + c // 2, 0, c), far) for c in range(CHUNKS)]
    to_band = {c: remote(mesh_ref.at[piece(c)], place(2 - c // 2, 1, c), band) for c in order}
    on_band = [remote(place(1, 0, c), place(3, 0, c), band) for c in (0, 1)]
    on_far = [remote(place(1, 1, c), place(3, 1, c), far) for c in (2, 3)]
    means = [
        remote(mean_w.at[0], mean_w.at[2], far),
        remote(mean_w.at[1], mean_w.at[3], band),
        remote(mean_w.at[1], mean_w.at[4], far),
        remote(mean_w.at[0], mean_w.at[5], band),
        remote(mean_w.at[0:2], mean_w.at[6:8], near),
    ]

    def share(start, size, target):
        source, target = pl.ds(start, size), pl.ds(target, size)
        return [
            remote(key_ref.at[source], key_ref.at[target], core),
            remote(value_ref.at[:, source], value_ref.at[:, target], core),
        ]

    shares = [
        share(0, NB, NB),
        share(2 * NB + HB, HB, 4 * NB + HB),
        share(3 * NB + HB, HB, 4 * NB),
    ]
    reads = [
        remote(read_w.at[0], read_w.at[slot], peer)
        for slot, peer in ((1, core), (2, far), (3, band), (4, band_core), (5, near))
    ]
    for c in (0, 1):
        to_far[c].start()
    to_band[2].start()

    for copy in smalls[1:3]:
        copy.wait()
    build_enc(enc_src_ref[...], enc_count_ref[...], lat, parity, enc_lo, enc_hi, enc_onehot, enc_pick)
    for copy in grids[:2]:
        copy.wait_recv()
    build_enc(peer_src[...], peer_count[...], lat, parity, enc_lo, enc_hi, enc_onehot, peer_pick)
    summed = dot(flat_ref[...], enc_pick[0:main, :])
    for copy in grids[2:]:
        copy.wait_recv()
    part_out[...] = dot(flat_ref[...], peer_pick[0:main, :]) + dot(halo_ref[...], peer_pick[main:, :])
    summed = summed + dot(halo_ref[...], enc_pick[main:, :])
    part.start()
    to_band[3].start()
    to_band[2].wait_recv()
    on_far[0].start()
    for h in range(HEADS):
        for first, last in ((0, 1), (2, 4), (5, 6)):
            value_ref[h * VROWS + HEAD : (h + 1) * VROWS, first * NB : last * NB] = jnp.ones(
                (VROWS - HEAD, (last - first) * NB), bf16
            )
    for copy in smalls[3:8]:
        copy.wait()
    build_mask(nbr_ref[...], nbr_count_ref[...], lat, lon, inner, nbr_hi, nbr_lo, bias_ref)
    build_dec(dec_src_ref, lat, lon, inner, dec_pick)
    part.wait_recv()
    mean = ((summed + part_in[...]) / enc_count_ref[...].astype(f32)).astype(bf16)
    mean_w[0] = mean[:, :HB]
    mean_w[1] = mean[:, HB:]
    own_load.wait()
    for copy in means:
        copy.start()
    for c in (0, 1):
        to_far[c + 2].start()
        to_band[c].start()
    for c in (0, 1):
        to_far[c].wait_recv()
        on_band[c].start()
    for load in loads[:3]:
        load.wait()
    for load in loads[4:]:
        load.start()

    def phase_loop(phase, carry):
        def block(i, carry):
            step = 2 * phase + i

            @pl.when(step == 1)
            def _():
                to_band[3].wait_recv()
                on_far[1].start()
                for copy in shares[0]:
                    copy.start()
                for copy in means[:2]:
                    copy.wait_recv()

            @pl.when(step == 2)
            def _():
                for copy in means[2:4] + [to_far[2], to_far[3], to_band[0], to_band[1]]:
                    copy.wait_recv()
                for copy in shares[1]:
                    copy.start()

            @pl.when(step == 3)
            def _():
                means[4].wait_recv()
                for copy in shares[2]:
                    copy.start()
                for copy in on_band + on_far:
                    copy.wait_recv()

            unit_mean = jnp.concatenate([mean_w[2 * step], mean_w[2 * step + 1]], axis=1)
            embedded = silu(
                lax.dot_general(
                    unit_mean, w_embed_ref[...], (((0,), (0,)), ((), ())), preferred_element_type=f32
                )
            ).astype(bf16)
            latent = mesh_w[step].astype(f32) + dot(embedded, weights[0])
            normed = layer_norm(latent, gain_attn_ref[...]).astype(bf16)
            rows = pl.ds(pl.multiple_of(jnp.where(step == 3, 5, step + jnp.minimum(step, 1)) * NB, NB), NB)
            key_ref[rows, :] = dot(normed, weights[1]).astype(bf16)
            values = dot(normed, weights[2]).T.astype(bf16)
            for h in range(HEADS):
                value_ref[h * VROWS : h * VROWS + HEAD, rows] = values[h * HEAD : (h + 1) * HEAD, :]

            @pl.when(step == 0)
            def _():
                latent_ref[...] = latent
                loads[3].wait()
                query_ref[...] = (dot(normed, weights[3]).astype(bf16).astype(f32) * 0.125).astype(bf16)

            return carry

        lax.fori_loop(0, 2, block, 0)

        @pl.when(phase == 0)
        def _():
            for copy in shares[0]:
                copy.wait_recv()

        @pl.when(phase == 1)
        def _():
            for copy in shares[1] + shares[2]:
                copy.wait_recv()

        attention(
            phase,
            query_ref,
            key_ref,
            value_ref,
            bias_ref,
            (score_a, score_b),
            (expo_a, expo_b),
            sum_ref,
            peak_ref,
        )
        return carry

    lax.fori_loop(0, 2, phase_loop, 0)

    def merge(h, carry):
        peak_a = peak_ref[0, pl.ds(h, 1), :]
        peak_b = peak_ref[1, pl.ds(h, 1), :]
        peak = jnp.maximum(peak_a, peak_b)
        joined = sum_ref[0, h] * jnp.exp(peak_a - peak) + sum_ref[1, h] * jnp.exp(peak_b - peak)
        context_ref[pl.ds(pl.multiple_of(h * HEAD, HEAD), HEAD), :] = (
            joined[0:HEAD, :] / joined[HEAD : HEAD + 1, :]
        ).astype(bf16)
        return carry

    lax.fori_loop(0, HEADS, merge, 0)
    for load in loads[4:] + smalls[8:]:
        load.wait()
    mixed = latent_ref[...] + lax.dot_general(
        context_ref[...], weights[4], (((0,), (0,)), ((), ())), preferred_element_type=f32
    )
    normed_out = layer_norm(mixed, gain_dec_ref[...]).astype(bf16)
    decoded = silu(dot(normed_out, weights[5])).astype(bf16)
    read_w[0] = lax.dot_general(
        w_readout_ref[...], decoded, (((1,), (1,)), ((), ())), preferred_element_type=f32
    ).astype(bf16)
    for copy in reads:
        copy.start()

    def add_slots(slots, first, last):
        def chunk(c, carry):
            lanes = pl.ds(pl.multiple_of(c * NB, NB), NB)
            update = sum(dot(read_w[b], dec_pick[c, b * NB : (b + 1) * NB, :]) for b in slots)
            if not first:
                update = update + total_ref[:, lanes]
            if last:
                update = flat_ref[:, lanes].astype(f32) + update / 3.0
                out_ref[:, 2 * c, :] = update[:, :COLS]
                out_ref[:, 2 * c + 1, :] = update[:, COLS:]
            else:
                total_ref[:, lanes] = update
            return carry

        lax.fori_loop(0, main // NB, chunk, 0)

    add_slots((0,), True, False)
    reads[0].wait_recv()
    add_slots((1,), False, False)
    for copy in reads[1:]:
        copy.wait_recv()
    add_slots((2, 3, 4, 5), False, True)
    blocks = to_far + list(to_band.values()) + on_band + on_far
    for copy in grids + [part] + blocks + means + shares[0] + shares[1] + shares[2] + reads:
        copy.wait_send()


def body(
    grid_state,
    mesh_feat,
    enc_src,
    enc_count,
    nbr_ids,
    nbr_count,
    dec_src,
    w_embed,
    w_encode,
    w_query,
    w_key,
    w_value,
    w_output,
    w_decode,
    w_readout,
    norm_attn,
    norm_dec,
):
    main = ROWS * COLS
    vmem = pl.BlockSpec(memory_space=pltpu.VMEM)
    hbm = pl.BlockSpec(memory_space=pl.ANY)
    out = pl.pallas_call(
        kernel,
        out_shape=pltpu.VMEM((V, ROWS, COLS), f32),
        in_specs=[hbm] * 17,
        out_specs=vmem,
        scratch_shapes=[
            pltpu.VMEM((V, ROWS, COLS), bf16),
            pltpu.VMEM((KE, NB), i32),
            pltpu.VMEM((1, NB), i32),
            pltpu.VMEM((KM, NB), i32),
            pltpu.VMEM((1, NB), i32),
            pltpu.VMEM((3, ROWS, COLS), i32),
            pltpu.VMEM((V, D), bf16),
            pltpu.VMEM((V, D), bf16),
            pltpu.VMEM((1, D), f32),
            pltpu.VMEM((1, D), f32),
            pltpu.VMEM((V, main), bf16),
            pltpu.VMEM((V, 2 * ROWS * HALO), bf16),
            pltpu.VMEM((V, 2 * ROWS * HALO), bf16),
            pltpu.VMEM((KE, NB), i32),
            pltpu.VMEM((1, NB), i32),
            pltpu.VMEM((V, NB), f32),
            pltpu.VMEM((V, NB), f32),
            pltpu.VMEM((V, main), f32),
            pltpu.VMEM((4, NB, D), bf16),
            pltpu.VMEM((8, V, HB), bf16),
            pltpu.VMEM((SLOTS, V, NB), bf16),
            pltpu.VMEM((6, D, D), bf16),
            pltpu.VMEM((KE, NB), i32),
            pltpu.VMEM((KE, NB), i32),
            pltpu.VMEM((KE * 16, NB), i32),
            pltpu.VMEM((20 * COLS, NB), bf16),
            pltpu.VMEM((20 * COLS, NB), bf16),
            pltpu.VMEM((KM, NB), i32),
            pltpu.VMEM((KM, NB), i32),
            pltpu.VMEM((WINDOW, NB), f32),
            pltpu.VMEM((8, WINDOW, NB), bf16),
            pltpu.VMEM((NB, D), f32),
            pltpu.VMEM((NB, D), bf16),
            pltpu.VMEM((WINDOW, D), bf16),
            pltpu.VMEM((HEADS * VROWS, WINDOW), bf16),
            pltpu.VMEM((HALF, NB), f32),
            pltpu.VMEM((HALF, NB), f32),
            pltpu.VMEM((HALF, NB), bf16),
            pltpu.VMEM((HALF, NB), bf16),
            pltpu.VMEM((2, HEADS, VROWS, NB), f32),
            pltpu.VMEM((2, HEADS, NB), f32),
            pltpu.VMEM((D, NB), bf16),
            pltpu.SemaphoreType.DMA((17,)),
            pltpu.SemaphoreType.DMA((64,)),
            pltpu.SemaphoreType.DMA((64,)),
        ],
        compiler_params=pltpu.CompilerParams(
            collective_id=0, has_side_effects=True, vmem_limit_bytes=VMEM_BYTES
        ),
        name="denoise",
    )(
        grid_state,
        mesh_feat,
        enc_src,
        enc_count.reshape(1, NB),
        nbr_ids,
        nbr_count.reshape(1, NB),
        dec_src,
        w_embed,
        w_encode,
        w_query,
        w_key,
        w_value,
        w_output,
        w_decode,
        w_readout.T,
        norm_attn.reshape(1, D),
        norm_dec.reshape(1, D),
    )
    return out


def solution(mesh):
    in_specs = (
        P(None, "lat", "lon"),
        P(("lat", "lon"), None),
        P(None, ("lat", "lon")),
        P(("lat", "lon")),
        P(None, ("lat", "lon")),
        P(("lat", "lon")),
        P(None, "lat", "lon"),
    ) + (P(),) * 10
    return jax.shard_map(
        body, mesh=mesh, in_specs=in_specs, out_specs=P(None, "lat", "lon"), check_vma=False
    )
```
